256 devices in a mesh: aux: 8 (over x_lo, y), occ: 32 (over x_hi, z, core).
Axes of the slice: x: 4 (x_hi: 2, x_lo: 2; x = x_hi * 2 + x_lo), y: 4, z: 8, core: 2. Of those that a mesh axis runs over, the one named last changes fastest.
Arguments:
- factor: bfloat16 [6144, 32, 1536], P('aux', 'occ'), may hold values from -0.67578125 to 0.67578125
- occ_energy: float32 [1024], replicated, may hold values from -3 to -0.5
- vir_energy: float32 [3072], replicated, may hold values from 0.5 to 4
- occ_pick: int32 [32], replicated, may hold values from 0 to 1023
- vir_pick: int32 [1536], replicated, may hold values from 0 to 3071
Outputs:
- gamma: float32 [6144, 32, 1536], P('aux', 'occ')
The draws below stay inside these ranges and needn't reach their ends.
All inputs are finite; a program needn't handle non-finite values.
Results may differ from the reference program's by a relative error of at most 0.0024.
Values may be sent and summed in bfloat16 or wider, within the bound.
A program may use at most 192 MiB of HBM per device.

```python
import jax
import jax.numpy as jnp
from jax import lax

NAUX = 6144
V = 1536
NOCC_ALL = 1024
NVIR_ALL = 3072
OCC_DEV = 1
OCC = 32
N_OCC = 32


def place_ends(entries, rng, low, top_value):
    shape = entries.shape
    spot = [jax.random.randint(jax.random.fold_in(rng, axis), (), 0, shape[axis]) for axis in range(len(shape))]
    entries = entries.at[tuple(spot)].set(low)
    longest = shape.index(max(shape))
    spot[longest] = (spot[longest] + 1) % shape[longest]
    return entries.at[tuple(spot)].set(top_value)


def shard_levels(stream_key, dims, pieces, least, top_value):
    def one(dim, shards_of):
        draws = jax.random.uniform(jax.random.fold_in(jax.random.fold_in(stream_key, 6), dim), (shards_of,), jnp.float32, least / len(pieces), top_value / len(pieces))
        return jnp.repeat(jnp.exp(draws), dims[dim] // shards_of).reshape((-1,) + (1,) * (len(dims) - dim - 1))

    factor_of = one(*pieces[0])
    for cut in pieces[1:]:
        factor_of = factor_of * one(*cut)
    return factor_of


def gaussian(stream_key, shape, scale, bound, pieces=(), held_as=jnp.bfloat16):
    drawn = scale * jax.random.normal(stream_key, shape, jnp.float32)
    if pieces:
        drawn = drawn * shard_levels(stream_key, shape, pieces, -0.22, 0.18)
    return jnp.clip(drawn, -bound, bound).astype(held_as)


def setup_inputs(seed: int = 0) -> dict:
    keys = jax.random.split(jax.random.key(seed), 6)
    return {
        "factor": gaussian(keys[0], (NAUX, OCC, V), (NAUX ** -0.25), 0.67578125, ((0, 8), (1, 32))),
        "occ_energy": jnp.clip(jax.random.uniform(keys[1], (NOCC_ALL,), jnp.float32, -3.0, -0.5), -3.0, -0.5),
        "vir_energy": jnp.clip(jax.random.uniform(keys[2], (NVIR_ALL,), jnp.float32, 0.5, 4.0), 0.5, 4.0),
        "occ_pick": place_ends(jax.random.randint(keys[3], (OCC,), 0, NOCC_ALL), jax.random.fold_in(keys[3], 1), 0, NOCC_ALL - 1).astype(jnp.int32),
        "vir_pick": place_ends(jax.random.randint(keys[4], (V,), 0, NVIR_ALL), jax.random.fold_in(keys[4], 1), 0, NVIR_ALL - 1).astype(jnp.int32),
    }


def reference(factor, occ_energy, vir_energy, occ_pick, vir_pick):
    occ_levels = occ_energy[occ_pick]
    vir_levels = vir_energy[vir_pick]

    def one_orbital(orbital):
        left_block = lax.dynamic_index_in_dim(factor, orbital, axis=1, keepdims=False)
        density = jnp.zeros((NAUX, V), jnp.float32)
        home = orbital // OCC_DEV
        for distance in (1, 2):
            for member in range(OCC_DEV):
                partner = (((home - distance) % N_OCC) * OCC_DEV + member).astype(jnp.int32)
                right_block = lax.dynamic_index_in_dim(factor, partner, axis=1, keepdims=False)
                integrals = lax.dot_general(left_block, right_block, (((0,), (0,)), ((), ())), preferred_element_type=jnp.float32)
                divisor = occ_levels[orbital] + occ_levels[partner] - vir_levels[:, None] - vir_levels[None, :]
                amplitudes = (integrals / divisor).astype(jnp.bfloat16)
                density = density + lax.dot_general(right_block, amplitudes, (((1,), (1,)), ((), ())), preferred_element_type=jnp.float32)
        return density

    stacked = lax.map(one_orbital, jnp.arange(OCC, dtype=jnp.int32))
    return jnp.transpose(stacked, (1, 0, 2))
```

```python
import functools

import jax
import jax.numpy as jnp
from jax import lax
from jax.experimental import pallas as pl
from jax.experimental.pallas import tpu as pltpu
from jax.sharding import PartitionSpec as P

MESH = pl.DeviceIdType.MESH
LANES = 128


def kernel(
    n_y, n_occ, f_ref, oe_ref, ve_ref, op_ref, vp_ref, out_ref,
    fx, ft, jj, jx, sb, rb, acc, tt, g1, vcol, vrow,
    g_s, g_r, z_s, z_r, s_s, s_r, rs_s, rs_r, ax_s, ax_r, a1_s, a1_r, a2_s, a2_r,
):
    rows, virt = f_ref.shape
    half = virt // 2
    chunk = virt // n_y
    sub = chunk // 2
    aux, occ = lax.axis_index("aux"), lax.axis_index("occ")
    h, y = aux // n_y, aux % n_y
    core = occ % 2

    def at_y(step):
        return {"aux": h * n_y + (y + step) % n_y}

    partner = {"aux": (1 - h) * n_y + y}
    sibling = {"occ": occ + 1 - 2 * core}
    ahead = {"occ": (occ + 2) % n_occ}
    behind = {"occ": (occ + n_occ - 2) % n_occ}

    def send(src, dst, s_sem, r_sem, where):
        return pltpu.make_async_remote_copy(
            src_ref=src, dst_ref=dst, send_sem=s_sem, recv_sem=r_sem,
            device_id=where, device_id_type=MESH,
        )

    def cols(start, size):
        return pl.ds(pl.multiple_of(start, LANES), size)

    mine, other = cols(h * half, half), cols((1 - h) * half, half)

    barrier = pltpu.get_barrier_semaphore()
    peers = [partner, sibling, ahead, behind] + [at_y(k) for k in range(1, n_y)]
    for peer in peers:
        pl.semaphore_signal(barrier, inc=1, device_id=peer, device_id_type=MESH)
    pl.semaphore_wait(barrier, len(peers))

    def gather(k, half_at):
        c = cols((half_at * (n_y // 2) + k) % n_y * chunk, chunk)
        return send(f_ref.at[:, c], fx.at[:, c], g_s.at[k], g_r.at[k], partner)

    for k in range(n_y):
        gather(k, 1 - h).start()

    ahead_parts = (
        send(f_ref.at[:, mine], jj.at[1, :, mine], z_s.at[0], z_r.at[0], ahead),
        send(fx.at[:, mine], jx.at[1], z_s.at[1], z_r.at[1], ahead),
        send(f_ref.at[:, other], jj.at[1, :, other], z_s.at[2], z_r.at[2], ahead),
    )
    down_parts = (
        send(f_ref.at[:, mine], jj.at[0, :, mine], s_s.at[0], s_r.at[0], sibling),
        send(fx.at[:, mine], jx.at[0], s_s.at[1], s_r.at[1], sibling),
        send(f_ref.at[:, other], jj.at[0, :, other], s_s.at[2], s_r.at[2], sibling),
    )
    up_parts = (
        send(jj.at[1, :, mine], jj.at[0, :, mine], s_s.at[0], s_r.at[0], sibling),
        send(jx.at[1], jx.at[0], s_s.at[1], s_r.at[1], sibling),
        send(jj.at[1, :, other], jj.at[0, :, other], s_s.at[2], s_r.at[2], sibling),
    )
    ahead_parts[0].start()

    @pl.when(core == 0)
    def _():
        down_parts[0].start()

    def turn(src, c, at):
        def body(t, carry):
            start = pl.multiple_of(c * chunk + t * LANES, LANES)
            ft[pl.ds(start, LANES), at * rows : (at + 1) * rows] = src[:, pl.ds(start, LANES)].T
            return carry

        lax.fori_loop(0, chunk // LANES, body, 0)

    def turn_own(k, carry):
        turn(f_ref, (h * (n_y // 2) + k) % n_y, 0)
        return carry

    lax.fori_loop(0, n_y, turn_own, 0)

    n_tiles = ve_ref.shape[0]
    lane = lax.broadcasted_iota(jnp.int32, (LANES, LANES), 1)

    def levels(g, carry):
        pick = jnp.broadcast_to(vp_ref[pl.ds(g, 1), :], (LANES, LANES)).T

        def one(m, total):
            energy = jnp.broadcast_to(ve_ref[pl.ds(m, 1), :], (LANES, LANES))
            return total + jnp.where(pick == lane + m * LANES, energy, 0.0)

        total = lax.fori_loop(0, n_tiles, one, jnp.zeros((LANES, LANES), jnp.float32))
        level = jnp.broadcast_to(jnp.sum(total, axis=1, keepdims=True), (LANES, LANES))
        start = pl.multiple_of(g * LANES, LANES)
        vcol[pl.ds(start, LANES), :] = level
        vrow[:, pl.ds(start, LANES)] = level.T[:8]
        return carry

    lax.fori_loop(0, virt // LANES, levels, 0)

    spot = lax.broadcasted_iota(jnp.int32, oe_ref.shape, 0) * LANES
    spot = spot + lax.broadcasted_iota(jnp.int32, oe_ref.shape, 1)

    def occ_level(orbital):
        found = jnp.where(spot == op_ref[orbital], oe_ref[...], 0.0)
        return jnp.sum(jnp.sum(found, axis=1, keepdims=True), axis=0, keepdims=True)

    def own_chunk(k):
        return (h * (n_y // 2) + k) % n_y

    def arrived(k):
        gather(k, h).wait_recv()
        turn(fx, own_chunk(k), 1)

    for k in range(n_y // 2):
        gather(k, h).wait_recv()
    ahead_parts[1].start()

    @pl.when(core == 0)
    def _():
        down_parts[1].start()
        down_parts[2].start()

    ahead_parts[2].start()
    for k in range(n_y // 2):
        turn(fx, own_chunk(k), 1)

    width = 256

    def partial_integrals(s, c):
        r = (c + n_y - y) % n_y
        a_rows = pl.ds(pl.multiple_of(c * chunk, chunk), chunk)

        def body(t, carry):
            start = pl.multiple_of(t * width, width)
            b_cols = cols(h * half + start, width)
            total = jnp.dot(
                ft[a_rows, :rows], jj[s, :, b_cols], preferred_element_type=jnp.float32
            )
            total = total + jnp.dot(
                ft[a_rows, rows:], jx[s, :, pl.ds(start, width)],
                preferred_element_type=jnp.float32,
            )

            @pl.when(r == 0)
            def _():
                acc[s, :, pl.ds(start, width)] = total

            @pl.when(r != 0)
            def _():
                sb[s, r - 1, :, pl.ds(start, width)] = total.astype(jnp.bfloat16)

            return carry

        lax.fori_loop(0, half // width, body, 0)

        @pl.when(r != 0)
        def _():
            send(
                sb.at[s, r - 1], rb.at[s, n_y - 1 - r], rs_s.at[s, r - 1],
                rs_r.at[s, n_y - 1 - r], {"aux": h * n_y + c},
            ).start()

    my_rows = pl.ds(pl.multiple_of(y * chunk, chunk), chunk)

    def finish(s):
        for k in range(n_y - 1):
            send(
                sb.at[s, k], rb.at[s, k], rs_s.at[s, k], rs_r.at[s, k], at_y(1)
            ).wait_recv()
        level = occ_level(occ) + occ_level((occ + n_occ - 1 - s) % n_occ)

        def body(t, carry):
            at = pl.ds(pl.multiple_of(t * 64, 64), 64)
            left = level - vcol[pl.ds(pl.multiple_of(y * chunk + t * 64, 64), 64), :]

            def inner(u, carry):
                c = pl.ds(pl.multiple_of(u * LANES, LANES), LANES)
                there = cols(h * half + u * LANES, LANES)
                total = acc[s, at, c]
                for k in range(n_y - 1):
                    total = total + rb[s, k, at, c].astype(jnp.float32)
                divisor = left - vrow[:1, there]
                tt[s, pl.ds(pl.multiple_of(y * chunk + t * 64, 64), 64), there] = (
                    total / divisor
                ).astype(jnp.bfloat16)
                return carry

            return lax.fori_loop(0, half // LANES, inner, carry)

        lax.fori_loop(0, chunk // 64, body, 0)

    def block(s, y_at, which, lo=0, size=None):
        start = pl.multiple_of((y + y_at + n_y) % n_y * chunk + lo, sub)
        return tt.at[s, pl.ds(start, size or chunk), mine if which == 0 else other]

    def across(s):
        part = block(s, 0, 0)
        return send(part, part, ax_s.at[s], ax_r.at[s], partner)

    def along(s, which, way):
        part = block(s, 0, which)
        return send(part, part, a1_s.at[s, which, way], a1_r.at[s, which, way], at_y(1 if way == 0 else n_y - 1))

    def onward(s, which, way):
        part = block(s, -1 if way == 0 else 1, which, 0 if way == 0 else sub, sub)
        return send(part, part, a2_s.at[s, which, way], a2_r.at[s, which, way], at_y(1 if way == 0 else n_y - 1))

    def spread_own(s):
        across(s).start()
        along(s, 0, 0).start()
        along(s, 0, 1).start()

    def spread_partner(s):
        across(s).wait_recv()
        along(s, 1, 0).start()
        along(s, 1, 1).start()

    def forward(s, which):
        for way in (0, 1):
            along(s, which, way).wait_recv()
            onward(s, which, way).start()

    def gathered(s):
        for which in (0, 1):
            for way in (0, 1):
                onward(s, which, way).wait_recv()

    first, second = 1 - core, core

    def wait_factors(s, part):
        @pl.when(s == 1)
        def _():
            ahead_parts[part].wait_recv()

        @pl.when(s == 0)
        def _():
            down_parts[part].wait_recv()

    def relay(part):
        @pl.when(core == 1)
        def _():
            ahead_parts[part].wait_recv()
            up_parts[part].start()

    wait_factors(first, 0)
    wait_factors(first, 1)
    for k in range(n_y):
        if k >= n_y // 2:
            arrived(k)
        partial_integrals(first, own_chunk(k))
        if k == 1:
            relay(0)
    relay(1)
    relay(2)
    finish(first)
    spread_own(first)

    @pl.when(core == 0)
    def _():
        wait_factors(second, 0)
        wait_factors(second, 1)

    def rest(k, carry):
        partial_integrals(second, (y + k) % n_y)
        return carry

    lax.fori_loop(1, n_y + 1, rest, 0)
    spread_partner(first)
    forward(first, 0)
    forward(first, 1)
    finish(second)
    spread_own(second)
    gathered(first)
    wait_factors(first, 2)

    def density(s, t):
        a_rows = pl.ds(pl.multiple_of(t * width, width), width)
        return lax.dot_general(
            jj[s], tt[s, a_rows, :], (((1,), (1,)), ((), ())), preferred_element_type=jnp.float32
        )

    def first_density(t, carry):
        g1[:, pl.ds(pl.multiple_of(t * width, width), width)] = density(first, t)
        return carry

    spread_partner(second)
    forward(second, 0)
    lax.fori_loop(0, virt // width, first_density, 0)
    forward(second, 1)

    @pl.when(core == 0)
    def _():
        wait_factors(second, 2)

    gathered(second)
    per_row = virt // LANES

    def last_density(t, carry):
        total = density(second, t) + g1[:, pl.ds(pl.multiple_of(t * width, width), width)]
        for u in range(width // LANES):
            out_ref[pl.ds(t * (width // LANES) + u, rows, stride=per_row), :] = total[
                :, u * LANES : (u + 1) * LANES
            ]
        return carry

    lax.fori_loop(0, virt // width, last_density, 0)

    for k in range(n_y):
        gather(k, 1 - h).wait_send()
    for part in range(3):
        ahead_parts[part].wait_send()
        down_parts[part].wait_send()
    for s in (0, 1):
        for k in range(n_y - 1):
            send(
                sb.at[s, k], rb.at[s, k], rs_s.at[s, k], rs_r.at[s, k], at_y(1)
            ).wait_send()
        across(s).wait_send()
        for which in (0, 1):
            for way in (0, 1):
                along(s, which, way).wait_send()
                onward(s, which, way).wait_send()


def on_device(factor, occ_energy, vir_energy, occ_pick, vir_pick):
    n_aux, n_occ = lax.axis_size("aux"), lax.axis_size("occ")
    n_y = n_aux // 2
    rows, _, virt = factor.shape
    half, chunk = virt // 2, virt // n_y
    bf16, f32 = jnp.bfloat16, jnp.float32
    dma = pltpu.SemaphoreType.DMA
    vmem = pl.BlockSpec(memory_space=pltpu.VMEM)
    out = pl.pallas_call(
        functools.partial(kernel, n_y, n_occ),
        out_shape=jax.ShapeDtypeStruct((rows * virt // LANES, LANES), f32),
        in_specs=[vmem, vmem, vmem, pl.BlockSpec(memory_space=pltpu.SMEM), vmem],
        out_specs=vmem,
        scratch_shapes=[
            pltpu.VMEM((rows, virt), bf16),
            pltpu.VMEM((virt, 2 * rows), bf16),
            pltpu.VMEM((2, rows, virt), bf16),
            pltpu.VMEM((2, rows, half), bf16),
            pltpu.VMEM((2, n_y - 1, chunk, half), bf16),
            pltpu.VMEM((2, n_y - 1, chunk, half), bf16),
            pltpu.VMEM((2, chunk, half), f32),
            pltpu.VMEM((2, virt, virt), bf16),
            pltpu.VMEM((rows, virt), f32),
            pltpu.VMEM((virt, LANES), f32),
            pltpu.VMEM((8, virt), f32),
            dma((n_y,)), dma((n_y,)),
            dma((3,)), dma((3,)),
            dma((3,)), dma((3,)),
            dma((2, n_y - 1)), dma((2, n_y - 1)),
            dma((2,)), dma((2,)),
            dma((2, 2, 2)), dma((2, 2, 2)),
            dma((2, 2, 2)), dma((2, 2, 2)),
        ],
        compiler_params=pltpu.CompilerParams(
            collective_id=0, has_side_effects=True, vmem_limit_bytes=60 * 2**20
        ),
    )(
        factor.reshape(rows, virt),
        occ_energy.reshape(-1, LANES),
        vir_energy.reshape(-1, LANES),
        occ_pick,
        vir_pick.reshape(-1, LANES),
    )
    return out.reshape(rows, 1, virt)


def solution(mesh):
    placed = (P("aux", "occ", None), P(), P(), P(), P())
    return jax.shard_map(
        on_device, mesh=mesh, in_specs=placed, out_specs=P("aux", "occ", None), check_vma=False
    )
```

```python
import functools

import jax
import jax.numpy as jnp
from jax import lax
from jax.experimental import pallas as pl
from jax.experimental.pallas import tpu as pltpu
from jax.sharding import PartitionSpec as P

MESH = pl.DeviceIdType.MESH
LANES = 128


def kernel(
    n_y, n_occ, f_ref, oe_ref, ve_ref, op_ref, vp_ref, out_ref,
    fx, ft, jj, jx, sb, rb, acc, tt, g1, vcol, vrow,
    g_s, g_r, z_s, z_r, w_s, w_r, q_s, q_r, s_s, s_r, rs_s, rs_r, ax_s, ax_r, a1_s, a1_r, a2_s, a2_r,
):
    rows, virt = f_ref.shape
    half = virt // 2
    chunk = virt // n_y
    sub = chunk // 2
    aux, occ = lax.axis_index("aux"), lax.axis_index("occ")
    h, y = aux // n_y, aux % n_y
    core = occ % 2

    def at_y(step):
        return {"aux": h * n_y + (y + step) % n_y}

    partner = {"aux": (1 - h) * n_y + y}
    sibling = {"occ": occ + 1 - 2 * core}
    ahead = {"occ": (occ + 2) % n_occ}
    behind = {"occ": (occ + n_occ - 2) % n_occ}
    wraps = (occ + 2) % (n_occ // 2) < 2
    ahead_across = {"aux": (1 - h) * n_y + y, "occ": (occ + 2) % n_occ}
    facing = {"occ": (occ + n_occ // 2) % n_occ}
    column = occ // (n_occ // 2) * (n_occ // 2)
    up_column = {"occ": column + (occ + 2) % (n_occ // 2)}
    down_column = {"occ": column + (occ + n_occ // 2 - 2) % (n_occ // 2)}
    behind_across = {"aux": (1 - h) * n_y + y, "occ": (occ + n_occ - 2) % n_occ}

    def send(src, dst, s_sem, r_sem, where):
        return pltpu.make_async_remote_copy(
            src_ref=src, dst_ref=dst, send_sem=s_sem, recv_sem=r_sem,
            device_id=where, device_id_type=MESH,
        )

    def cols(start, size):
        return pl.ds(pl.multiple_of(start, LANES), size)

    mine, other = cols(h * half, half), cols((1 - h) * half, half)

    barrier = pltpu.get_barrier_semaphore()
    peers = [partner, sibling, ahead, behind, ahead_across, behind_across]
    peers = peers + [facing, up_column, down_column] + [at_y(k) for k in range(1, n_y)]
    for peer in peers:
        pl.semaphore_signal(barrier, inc=1, device_id=peer, device_id_type=MESH)
    pl.semaphore_wait(barrier, len(peers))

    def order(k, half_at):
        per_half = n_y // 2
        return (half_at + k // per_half) % 2 * per_half + (y + 1 + k) % per_half

    def gather(k, half_at):
        c = cols(order(k, half_at) * chunk, chunk)
        return send(f_ref.at[:, c], fx.at[:, c], g_s.at[k], g_r.at[k], partner)

    for k in range(n_y // 2):
        gather(k, 1 - h).start()

    @pl.when(core == 1)
    def _():
        for k in range(n_y // 2, n_y):
            gather(k, 1 - h).start()


    upper, lower = pl.ds(rows // 2, rows // 2), pl.ds(0, rows // 2)

    class Ahead:
        def __init__(self, part):
            c = mine if part == 0 else other
            self.direct = send(f_ref.at[lower, c], jj.at[1, lower, c], z_s.at[part], z_r.at[part], ahead)
            self.second = send(f_ref.at[upper, c], jj.at[1, upper, c], w_s.at[part], w_r.at[part], ahead)
            self.detour = send(f_ref.at[upper, c], jj.at[2, upper, c], w_s.at[part], q_r.at[part], facing)
            self.onward = send(jj.at[2, upper, c], jj.at[1, upper, c], q_s.at[part], w_r.at[part], up_column)

        def start(self):
            @pl.when(wraps)
            def _():
                self.detour.start()

            self.direct.start()

            @pl.when(jnp.logical_not(wraps))
            def _():
                self.second.start()

        def hand_on(self):
            @pl.when(wraps)
            def _():
                self.detour.wait_recv()
                self.onward.start()

        def wait_recv(self):
            self.direct.wait_recv()
            self.second.wait_recv()

        def wait_send(self):
            self.direct.wait_send()
            self.second.wait_send()

            @pl.when(wraps)
            def _():
                self.onward.wait_send()

    ahead_parts = (
        Ahead(0),
        send(fx.at[:, mine], jx.at[1], z_s.at[1], z_r.at[1], ahead),
        Ahead(2),
    )
    straight = send(f_ref.at[:, other], jx.at[1], z_s.at[1], z_r.at[1], ahead_across)

    down_parts = (
        send(f_ref.at[:, mine], jj.at[0, :, mine], s_s.at[0], s_r.at[0], sibling),
        send(fx.at[:, mine], jx.at[0], s_s.at[1], s_r.at[1], sibling),
        send(f_ref.at[:, other], jj.at[0, :, other], s_s.at[2], s_r.at[2], sibling),
    )
    up_parts = (
        send(jj.at[1, :, mine], jj.at[0, :, mine], s_s.at[0], s_r.at[0], sibling),
        send(jx.at[1], jx.at[0], s_s.at[1], s_r.at[1], sibling),
        send(jj.at[1, :, other], jj.at[0, :, other], s_s.at[2], s_r.at[2], sibling),
    )
    @pl.when(wraps)
    def _():
        straight.start()

    @pl.when(core == 1)
    def _():
        ahead_parts[0].start()

    @pl.when(core == 0)
    def _():
        down_parts[0].start()

    def turn(src, c, at):
        def body(t, carry):
            start = pl.multiple_of(c * chunk + t * LANES, LANES)
            ft[pl.ds(start, LANES), at * rows : (at + 1) * rows] = src[:, pl.ds(start, LANES)].T
            return carry

        lax.fori_loop(0, chunk // LANES, body, 0)

    def turn_own(k, carry):
        turn(f_ref, order(k, h), 0)
        return carry

    lax.fori_loop(0, n_y, turn_own, 0)

    n_tiles = ve_ref.shape[0]
    lane = lax.broadcasted_iota(jnp.int32, (LANES, LANES), 1)

    def levels(g, carry):
        pick = jnp.broadcast_to(vp_ref[pl.ds(g, 1), :], (LANES, LANES)).T

        def one(m, total):
            energy = jnp.broadcast_to(ve_ref[pl.ds(m, 1), :], (LANES, LANES))
            return total + jnp.where(pick == lane + m * LANES, energy, 0.0)

        total = lax.fori_loop(0, n_tiles, one, jnp.zeros((LANES, LANES), jnp.float32))
        level = jnp.broadcast_to(jnp.sum(total, axis=1, keepdims=True), (LANES, LANES))
        start = pl.multiple_of(g * LANES, LANES)
        vcol[pl.ds(start, LANES), :] = level
        vrow[:, pl.ds(start, LANES)] = level.T[:8]
        return carry

    lax.fori_loop(0, virt // LANES, levels, 0)

    spot = lax.broadcasted_iota(jnp.int32, oe_ref.shape, 0) * LANES
    spot = spot + lax.broadcasted_iota(jnp.int32, oe_ref.shape, 1)

    def occ_level(orbital):
        found = jnp.where(spot == op_ref[orbital], oe_ref[...], 0.0)
        return jnp.sum(jnp.sum(found, axis=1, keepdims=True), axis=0, keepdims=True)

    def own_chunk(k):
        return order(k, h)

    def arrived(k):
        gather(k, h).wait_recv()
        turn(fx, own_chunk(k), 1)

    for k in range(n_y // 2):
        gather(k, h).wait_recv()

    @pl.when(jnp.logical_not(wraps))
    def _():
        ahead_parts[1].start()

    @pl.when(core == 0)
    def _():
        down_parts[1].start()
        for k in range(n_y // 2, n_y):
            gather(k, 1 - h).start()
        down_parts[2].start()

        @pl.when(jnp.logical_not(wraps))
        def _():
            ahead_parts[0].start()

    for k in range(n_y // 2):
        turn(fx, own_chunk(k), 1)

    width = 256

    def partial_integrals(s, c):
        r = (c + n_y - y) % n_y
        a_rows = pl.ds(pl.multiple_of(c * chunk, chunk), chunk)

        def body(t, carry):
            start = pl.multiple_of(t * width, width)
            b_cols = cols(h * half + start, width)
            total = jnp.dot(
                ft[a_rows, :rows], jj[s, :, b_cols], preferred_element_type=jnp.float32
            )
            total = total + jnp.dot(
                ft[a_rows, rows:], jx[s, :, pl.ds(start, width)],
                preferred_element_type=jnp.float32,
            )

            @pl.when(r == 0)
            def _():
                acc[s, :, pl.ds(start, width)] = total

            @pl.when(r != 0)
            def _():
                sb[s, r - 1, :, pl.ds(start, width)] = total.astype(jnp.bfloat16)

            return carry

        lax.fori_loop(0, half // width, body, 0)

        @pl.when(r != 0)
        def _():
            send(
                sb.at[s, r - 1], rb.at[s, n_y - 1 - r], rs_s.at[s, r - 1],
                rs_r.at[s, n_y - 1 - r], {"aux": h * n_y + c},
            ).start()

    my_rows = pl.ds(pl.multiple_of(y * chunk, chunk), chunk)

    def finish(s):
        for k in range(n_y - 1):
            send(
                sb.at[s, k], rb.at[s, k], rs_s.at[s, k], rs_r.at[s, k], at_y(1)
            ).wait_recv()
        level = occ_level(occ) + occ_level((occ + n_occ - 1 - s) % n_occ)

        def body(t, carry):
            at = pl.ds(pl.multiple_of(t * 64, 64), 64)
            left = level - vcol[pl.ds(pl.multiple_of(y * chunk + t * 64, 64), 64), :]

            def inner(u, carry):
                c = pl.ds(pl.multiple_of(u * LANES, LANES), LANES)
                there = cols(h * half + u * LANES, LANES)
                total = acc[s, at, c]
                for k in range(n_y - 1):
                    total = total + rb[s, k, at, c].astype(jnp.float32)
                divisor = left - vrow[:1, there]
                tt[s, pl.ds(pl.multiple_of(y * chunk + t * 64, 64), 64), there] = (
                    total / divisor
                ).astype(jnp.bfloat16)
                return carry

            return lax.fori_loop(0, half // LANES, inner, carry)

        lax.fori_loop(0, chunk // 64, body, 0)

    def block(s, y_at, which, lo=0, size=None):
        start = pl.multiple_of((y + y_at + n_y) % n_y * chunk + lo, sub)
        return tt.at[s, pl.ds(start, size or chunk), mine if which == 0 else other]

    def across(s):
        part = block(s, 0, 0)
        return send(part, part, ax_s.at[s], ax_r.at[s], partner)

    def along(s, which, way):
        part = block(s, 0, which)
        return send(part, part, a1_s.at[s, which, way], a1_r.at[s, which, way], at_y(1 if way == 0 else n_y - 1))

    def onward(s, which, way):
        part = block(s, -1 if way == 0 else 1, which, 0 if way == 0 else sub, sub)
        return send(part, part, a2_s.at[s, which, way], a2_r.at[s, which, way], at_y(1 if way == 0 else n_y - 1))

    def spread_own(s):
        across(s).start()
        along(s, 0, 0).start()
        along(s, 0, 1).start()

    def spread_partner(s):
        across(s).wait_recv()
        along(s, 1, 0).start()
        along(s, 1, 1).start()

    def forward(s, which):
        for way in (0, 1):
            along(s, which, way).wait_recv()
            onward(s, which, way).start()

    def gathered(s):
        for which in (0, 1):
            for way in (0, 1):
                onward(s, which, way).wait_recv()

    first, second = 0, 1

    def relay(part):
        @pl.when(core == 1)
        def _():
            ahead_parts[part].wait_recv()
            up_parts[part].start()

    def given(part):
        down_parts[part].wait_recv()

    @pl.when(core == 1)
    def _():
        given(0)
        given(1)
        for k in range(n_y // 2):
            partial_integrals(first, own_chunk(k))
        ahead_parts[0].hand_on()

    relay(0)
    for k in range(n_y // 2, n_y):
        arrived(k)

        @pl.when(core == 1)
        def _():
            partial_integrals(first, own_chunk(k))

    @pl.when((core == 0) & wraps)
    def _():
        ahead_parts[0].start()

    relay(1)

    def chunks(s):
        def body(k, carry):
            partial_integrals(s, (y + k) % n_y)
            return carry

        lax.fori_loop(1, n_y + 1, body, 0)

    @pl.when(core == 0)
    def _():
        given(0)
        given(1)
        chunks(first)
        ahead_parts[0].hand_on()

    @pl.when(core == 1)
    def _():
        chunks(second)

    finish(first)
    spread_own(first)

    @pl.when(core == 0)
    def _():
        ahead_parts[0].wait_recv()
        ahead_parts[1].wait_recv()
        chunks(second)

    ahead_parts[2].start()
    spread_partner(first)
    forward(first, 0)
    ahead_parts[2].hand_on()
    forward(first, 1)
    finish(second)
    spread_own(second)
    relay(2)
    gathered(first)
    given(2)

    def density(s, t):
        a_rows = pl.ds(pl.multiple_of(t * width, width), width)
        return lax.dot_general(
            jj[s], tt[s, a_rows, :], (((1,), (1,)), ((), ())), preferred_element_type=jnp.float32
        )

    def first_density(t, carry):
        g1[:, pl.ds(pl.multiple_of(t * width, width), width)] = density(first, t)
        return carry

    spread_partner(second)
    forward(second, 0)
    lax.fori_loop(0, virt // width, first_density, 0)
    forward(second, 1)

    @pl.when(core == 0)
    def _():
        ahead_parts[2].wait_recv()

    gathered(second)
    per_row = virt // LANES

    def last_density(t, carry):
        total = density(second, t) + g1[:, pl.ds(pl.multiple_of(t * width, width), width)]
        for u in range(width // LANES):
            out_ref[pl.ds(t * (width // LANES) + u, rows, stride=per_row), :] = total[
                :, u * LANES : (u + 1) * LANES
            ]
        return carry

    lax.fori_loop(0, virt // width, last_density, 0)

    for k in range(n_y):
        gather(k, 1 - h).wait_send()
    for part in range(3):
        ahead_parts[part].wait_send()
        down_parts[part].wait_send()
    for s in (0, 1):
        for k in range(n_y - 1):
            send(
                sb.at[s, k], rb.at[s, k], rs_s.at[s, k], rs_r.at[s, k], at_y(1)
            ).wait_send()
        across(s).wait_send()
        for which in (0, 1):
            for way in (0, 1):
                along(s, which, way).wait_send()
                onward(s, which, way).wait_send()


def on_device(factor, occ_energy, vir_energy, occ_pick, vir_pick):
    n_aux, n_occ = lax.axis_size("aux"), lax.axis_size("occ")
    n_y = n_aux // 2
    rows, _, virt = factor.shape
    half, chunk = virt // 2, virt // n_y
    bf16, f32 = jnp.bfloat16, jnp.float32
    dma = pltpu.SemaphoreType.DMA
    vmem = pl.BlockSpec(memory_space=pltpu.VMEM)
    out = pl.pallas_call(
        functools.partial(kernel, n_y, n_occ),
        out_shape=jax.ShapeDtypeStruct((rows * virt // LANES, LANES), f32),
        in_specs=[vmem, vmem, vmem, pl.BlockSpec(memory_space=pltpu.SMEM), vmem],
        out_specs=vmem,
        scratch_shapes=[
            pltpu.VMEM((rows, virt), bf16),
            pltpu.VMEM((virt, 2 * rows), bf16),
            pltpu.VMEM((3, rows, virt), bf16),
            pltpu.VMEM((2, rows, half), bf16),
            pltpu.VMEM((2, n_y - 1, chunk, half), bf16),
            pltpu.VMEM((2, n_y - 1, chunk, half), bf16),
            pltpu.VMEM((2, chunk, half), f32),
            pltpu.VMEM((2, virt, virt), bf16),
            pltpu.VMEM((rows, virt), f32),
            pltpu.VMEM((virt, LANES), f32),
            pltpu.VMEM((8, virt), f32),
            dma((n_y,)), dma((n_y,)),
            dma((3,)), dma((3,)),
            dma((3,)), dma((3,)),
            dma((3,)), dma((3,)),
            dma((3,)), dma((3,)),
            dma((2, n_y - 1)), dma((2, n_y - 1)),
            dma((2,)), dma((2,)),
            dma((2, 2, 2)), dma((2, 2, 2)),
            dma((2, 2, 2)), dma((2, 2, 2)),
        ],
        compiler_params=pltpu.CompilerParams(
            collective_id=0, has_side_effects=True, vmem_limit_bytes=60 * 2**20
        ),
    )(
        factor.reshape(rows, virt),
        occ_energy.reshape(-1, LANES),
        vir_energy.reshape(-1, LANES),
        occ_pick,
        vir_pick.reshape(-1, LANES),
    )
    return out.reshape(rows, 1, virt)


def solution(mesh):
    placed = (P("aux", "occ", None), P(), P(), P(), P())
    return jax.shard_map(
        on_device, mesh=mesh, in_specs=placed, out_specs=P("aux", "occ", None), check_vma=False
    )
```

```python
import functools

import jax
import jax.numpy as jnp
from jax import lax
from jax.experimental import pallas as pl
from jax.experimental.pallas import tpu as pltpu
from jax.sharding import PartitionSpec as P

MESH = pl.DeviceIdType.MESH
LANES = 128


def kernel(
    n_y, n_occ, f_ref, oe_ref, ve_ref, op_ref, vp_ref, out_ref,
    fx, ft, jj, jx, sb, rb, acc, tt, g1, vcol, vrow,
    g_s, g_r, z_s, z_r, w_s, w_r, q_s, q_r, s_s, s_r, rs_s, rs_r, ax_s, ax_r, af_s, af_r, a1_s, a1_r, a2_s, a2_r,
):
    rows, virt = f_ref.shape
    half = virt // 2
    chunk = virt // n_y
    sub = chunk // 2
    aux, occ = lax.axis_index("aux"), lax.axis_index("occ")
    h, y = aux // n_y, aux % n_y
    core = occ % 2

    def at_y(step):
        return {"aux": h * n_y + (y + step) % n_y}

    partner = {"aux": (1 - h) * n_y + y}
    sibling = {"occ": occ + 1 - 2 * core}
    ahead = {"occ": (occ + 2) % n_occ}
    behind = {"occ": (occ + n_occ - 2) % n_occ}
    wraps = (occ + 2) % (n_occ // 2) < 2
    ahead_across = {"aux": (1 - h) * n_y + y, "occ": (occ + 2) % n_occ}
    facing = {"occ": (occ + n_occ // 2) % n_occ}
    column = occ // (n_occ // 2) * (n_occ // 2)
    up_column = {"occ": column + (occ + 2) % (n_occ // 2)}
    down_column = {"occ": column + (occ + n_occ // 2 - 2) % (n_occ // 2)}
    behind_across = {"aux": (1 - h) * n_y + y, "occ": (occ + n_occ - 2) % n_occ}

    def send(src, dst, s_sem, r_sem, where):
        return pltpu.make_async_remote_copy(
            src_ref=src, dst_ref=dst, send_sem=s_sem, recv_sem=r_sem,
            device_id=where, device_id_type=MESH,
        )

    def cols(start, size):
        return pl.ds(pl.multiple_of(start, LANES), size)

    mine, other = cols(h * half, half), cols((1 - h) * half, half)

    barrier = pltpu.get_barrier_semaphore()
    peers = [partner, sibling, ahead, behind, ahead_across, behind_across]
    peers = peers + [facing, up_column, down_column] + [at_y(k) for k in range(1, n_y)]
    for peer in peers:
        pl.semaphore_signal(barrier, inc=1, device_id=peer, device_id_type=MESH)
    pl.semaphore_wait(barrier, len(peers))

    def order(k, half_at):
        per_half = n_y // 2
        return (half_at + k // per_half) % 2 * per_half + (y + 1 + k) % per_half

    def gather(k, half_at):
        c = cols(order(k, half_at) * chunk, chunk)
        return send(f_ref.at[:, c], fx.at[:, c], g_s.at[k], g_r.at[k], partner)

    for k in range(n_y // 2):
        gather(k, 1 - h).start()

    @pl.when(core == 1)
    def _():
        for k in range(n_y // 2, n_y):
            gather(k, 1 - h).start()


    upper, lower = pl.ds(rows // 2, rows // 2), pl.ds(0, rows // 2)

    class Ahead:
        def __init__(self, part):
            c = mine if part == 0 else other
            self.direct = send(f_ref.at[lower, c], jj.at[1, lower, c], z_s.at[part], z_r.at[part], ahead)
            self.second = send(f_ref.at[upper, c], jj.at[1, upper, c], w_s.at[part], w_r.at[part], ahead)
            self.detour = send(f_ref.at[upper, c], jj.at[2, upper, c], w_s.at[part], q_r.at[part], facing)
            self.onward = send(jj.at[2, upper, c], jj.at[1, upper, c], q_s.at[part], w_r.at[part], up_column)

        def start(self):
            @pl.when(wraps)
            def _():
                self.detour.start()

            self.direct.start()

            @pl.when(jnp.logical_not(wraps))
            def _():
                self.second.start()

        def hand_on(self):
            @pl.when(wraps)
            def _():
                self.detour.wait_recv()
                self.onward.start()

        def wait_recv(self):
            self.direct.wait_recv()
            self.second.wait_recv()

        def wait_send(self):
            self.direct.wait_send()
            self.second.wait_send()

            @pl.when(wraps)
            def _():
                self.onward.wait_send()

    ahead_parts = (
        Ahead(0),
        send(fx.at[:, mine], jx.at[1], z_s.at[1], z_r.at[1], ahead),
        Ahead(2),
    )
    straight = send(f_ref.at[:, other], jx.at[1], z_s.at[1], z_r.at[1], ahead_across)

    down_parts = (
        send(f_ref.at[:, mine], jj.at[0, :, mine], s_s.at[0], s_r.at[0], sibling),
        send(fx.at[:, mine], jx.at[0], s_s.at[1], s_r.at[1], sibling),
        send(f_ref.at[:, other], jj.at[0, :, other], s_s.at[2], s_r.at[2], sibling),
    )
    up_parts = (
        send(jj.at[1, :, mine], jj.at[0, :, mine], s_s.at[0], s_r.at[0], sibling),
        send(jx.at[1], jx.at[0], s_s.at[1], s_r.at[1], sibling),
        send(jj.at[1, :, other], jj.at[0, :, other], s_s.at[2], s_r.at[2], sibling),
    )
    @pl.when(wraps)
    def _():
        straight.start()

    @pl.when(core == 1)
    def _():
        ahead_parts[0].start()

    @pl.when(core == 0)
    def _():
        down_parts[0].start()

    def turn(src, c, at):
        def body(t, carry):
            start = pl.multiple_of(c * chunk + t * LANES, LANES)
            ft[pl.ds(start, LANES), at * rows : (at + 1) * rows] = src[:, pl.ds(start, LANES)].T
            return carry

        lax.fori_loop(0, chunk // LANES, body, 0)

    def turn_own(k, carry):
        turn(f_ref, order(k, h), 0)
        return carry

    lax.fori_loop(0, n_y, turn_own, 0)

    n_tiles = ve_ref.shape[0]
    lane = lax.broadcasted_iota(jnp.int32, (LANES, LANES), 1)

    def levels(g, carry):
        pick = jnp.broadcast_to(vp_ref[pl.ds(g, 1), :], (LANES, LANES)).T

        def one(m, total):
            energy = jnp.broadcast_to(ve_ref[pl.ds(m, 1), :], (LANES, LANES))
            return total + jnp.where(pick == lane + m * LANES, energy, 0.0)

        total = lax.fori_loop(0, n_tiles, one, jnp.zeros((LANES, LANES), jnp.float32))
        level = jnp.broadcast_to(jnp.sum(total, axis=1, keepdims=True), (LANES, LANES))
        start = pl.multiple_of(g * LANES, LANES)
        vcol[pl.ds(start, LANES), :] = level
        vrow[:, pl.ds(start, LANES)] = level.T[:8]
        return carry

    lax.fori_loop(0, virt // LANES, levels, 0)

    spot = lax.broadcasted_iota(jnp.int32, oe_ref.shape, 0) * LANES
    spot = spot + lax.broadcasted_iota(jnp.int32, oe_ref.shape, 1)

    def occ_level(orbital):
        found = jnp.where(spot == op_ref[orbital], oe_ref[...], 0.0)
        return jnp.sum(jnp.sum(found, axis=1, keepdims=True), axis=0, keepdims=True)

    def own_chunk(k):
        return order(k, h)

    def arrived(k):
        gather(k, h).wait_recv()
        turn(fx, own_chunk(k), 1)

    for k in range(n_y // 2):
        gather(k, h).wait_recv()

    @pl.when(jnp.logical_not(wraps))
    def _():
        ahead_parts[1].start()

    @pl.when(core == 0)
    def _():
        down_parts[1].start()
        for k in range(n_y // 2, n_y):
            gather(k, 1 - h).start()
        down_parts[2].start()

        ahead_parts[0].start()

    @pl.when(core == 1)
    def _():
        ahead_parts[0].hand_on()

    for k in range(n_y // 2):
        turn(fx, own_chunk(k), 1)

    width = 256

    def partial_integrals(s, c):
        r = (c + n_y - y) % n_y
        a_rows = pl.ds(pl.multiple_of(c * chunk, chunk), chunk)

        def body(t, carry):
            start = pl.multiple_of(t * width, width)
            b_cols = cols(h * half + start, width)
            total = jnp.dot(
                ft[a_rows, :rows], jj[s, :, b_cols], preferred_element_type=jnp.float32
            )
            total = total + jnp.dot(
                ft[a_rows, rows:], jx[s, :, pl.ds(start, width)],
                preferred_element_type=jnp.float32,
            )

            @pl.when(r == 0)
            def _():
                acc[s, :, pl.ds(start, width)] = total

            @pl.when(r != 0)
            def _():
                sb[s, r - 1, :, pl.ds(start, width)] = total.astype(jnp.bfloat16)

            return carry

        lax.fori_loop(0, half // width, body, 0)

        @pl.when(r != 0)
        def _():
            send(
                sb.at[s, r - 1], rb.at[s, n_y - 1 - r], rs_s.at[s, r - 1],
                rs_r.at[s, n_y - 1 - r], {"aux": h * n_y + c},
            ).start()

    my_rows = pl.ds(pl.multiple_of(y * chunk, chunk), chunk)

    def finish(s):
        for k in range(n_y - 1):
            send(
                sb.at[s, k], rb.at[s, k], rs_s.at[s, k], rs_r.at[s, k], at_y(1)
            ).wait_recv()
        level = occ_level(occ) + occ_level((occ + n_occ - 1 - s) % n_occ)

        def body(t, carry):
            at = pl.ds(pl.multiple_of(t * 64, 64), 64)
            left = level - vcol[pl.ds(pl.multiple_of(y * chunk + t * 64, 64), 64), :]

            def inner(u, carry):
                c = pl.ds(pl.multiple_of(u * LANES, LANES), LANES)
                there = cols(h * half + u * LANES, LANES)
                total = acc[s, at, c]
                for k in range(n_y - 1):
                    total = total + rb[s, k, at, c].astype(jnp.float32)
                divisor = left - vrow[:1, there]
                tt[s, pl.ds(pl.multiple_of(y * chunk + t * 64, 64), 64), there] = (
                    total / divisor
                ).astype(jnp.bfloat16)
                return carry

            return lax.fori_loop(0, half // LANES, inner, carry)

        lax.fori_loop(0, chunk // 64, body, 0)

    def block(s, y_at, which, lo=0, size=None):
        start = pl.multiple_of((y + y_at + n_y) % n_y * chunk + lo, sub)
        return tt.at[s, pl.ds(start, size or chunk), mine if which == 0 else other]

    def across(s):
        part = block(s, 0, 0)
        return send(part, part, ax_s.at[s], ax_r.at[s], partner)

    def across_far(s):
        part = block(s, 2, 0)
        return send(part, part, af_s.at[s], af_r.at[s], partner)

    def along(s, which, way):
        part = block(s, 0, which)
        return send(part, part, a1_s.at[s, which, way], a1_r.at[s, which, way], at_y(1 if way == 0 else n_y - 1))

    def onward(s, way):
        part = block(s, -1 if way == 0 else 1, 0, 0 if way == 0 else sub, sub)
        return send(part, part, a2_s.at[s, way], a2_r.at[s, way], at_y(1 if way == 0 else n_y - 1))

    def spread_own(s):
        across(s).start()
        along(s, 0, 0).start()
        along(s, 0, 1).start()

    def spread_partner(s):
        across(s).wait_recv()
        along(s, 1, 0).start()
        along(s, 1, 1).start()

    def forward(s):
        for way in (0, 1):
            along(s, 0, way).wait_recv()
            onward(s, way).start()

    def spread_far(s):
        for way in (0, 1):
            onward(s, way).wait_recv()
        across_far(s).start()

    def gathered(s):
        for way in (0, 1):
            along(s, 1, way).wait_recv()
        across_far(s).wait_recv()

    first, second = 0, 1

    def relay(part):
        @pl.when(core == 1)
        def _():
            ahead_parts[part].wait_recv()
            up_parts[part].start()

    def given(part):
        down_parts[part].wait_recv()

    @pl.when(core == 1)
    def _():
        given(0)
        given(1)
        for k in range(n_y // 2):
            partial_integrals(first, own_chunk(k))

    for k in range(n_y // 2, n_y):
        arrived(k)

        @pl.when(core == 1)
        def _():
            partial_integrals(first, own_chunk(k))

    @pl.when(core == 0)
    def _():
        ahead_parts[0].hand_on()

    def chunks(s):
        def body(k, carry):
            partial_integrals(s, (y + k) % n_y)
            return carry

        lax.fori_loop(1, n_y + 1, body, 0)

    @pl.when(core == 0)
    def _():
        given(0)
        given(1)
        chunks(first)

    relay(0)
    relay(1)
    finish(first)
    spread_own(first)

    @pl.when(core == 1)
    def _():
        chunks(second)

    @pl.when(core == 0)
    def _():
        ahead_parts[0].wait_recv()
        ahead_parts[1].wait_recv()
        chunks(second)

    ahead_parts[2].start()
    forward(first)
    spread_partner(first)
    ahead_parts[2].hand_on()
    finish(second)
    spread_own(second)
    spread_far(first)
    relay(2)
    forward(second)
    spread_partner(second)
    gathered(first)
    given(2)

    def density(s, t):
        a_rows = pl.ds(pl.multiple_of(t * width, width), width)
        return lax.dot_general(
            jj[s], tt[s, a_rows, :], (((1,), (1,)), ((), ())), preferred_element_type=jnp.float32
        )

    def first_density(t, carry):
        g1[:, pl.ds(pl.multiple_of(t * width, width), width)] = density(first, t)
        return carry

    lax.fori_loop(0, virt // (2 * width), first_density, 0)
    spread_far(second)
    lax.fori_loop(virt // (2 * width), virt // width, first_density, 0)

    @pl.when(core == 0)
    def _():
        ahead_parts[2].wait_recv()

    gathered(second)
    per_row = virt // LANES

    def last_density(t, carry):
        total = density(second, t) + g1[:, pl.ds(pl.multiple_of(t * width, width), width)]
        for u in range(width // LANES):
            out_ref[pl.ds(t * (width // LANES) + u, rows, stride=per_row), :] = total[
                :, u * LANES : (u + 1) * LANES
            ]
        return carry

    lax.fori_loop(0, virt // width, last_density, 0)

    for k in range(n_y):
        gather(k, 1 - h).wait_send()
    for part in range(3):
        ahead_parts[part].wait_send()
        down_parts[part].wait_send()
    for s in (0, 1):
        for k in range(n_y - 1):
            send(
                sb.at[s, k], rb.at[s, k], rs_s.at[s, k], rs_r.at[s, k], at_y(1)
            ).wait_send()
        across(s).wait_send()
        across_far(s).wait_send()
        for way in (0, 1):
            along(s, 0, way).wait_send()
            along(s, 1, way).wait_send()
            onward(s, way).wait_send()


def on_device(factor, occ_energy, vir_energy, occ_pick, vir_pick):
    n_aux, n_occ = lax.axis_size("aux"), lax.axis_size("occ")
    n_y = n_aux // 2
    rows, _, virt = factor.shape
    half, chunk = virt // 2, virt // n_y
    bf16, f32 = jnp.bfloat16, jnp.float32
    dma = pltpu.SemaphoreType.DMA
    vmem = pl.BlockSpec(memory_space=pltpu.VMEM)
    out = pl.pallas_call(
        functools.partial(kernel, n_y, n_occ),
        out_shape=jax.ShapeDtypeStruct((rows * virt // LANES, LANES), f32),
        in_specs=[vmem, vmem, vmem, pl.BlockSpec(memory_space=pltpu.SMEM), vmem],
        out_specs=vmem,
        scratch_shapes=[
            pltpu.VMEM((rows, virt), bf16),
            pltpu.VMEM((virt, 2 * rows), bf16),
            pltpu.VMEM((3, rows, virt), bf16),
            pltpu.VMEM((2, rows, half), bf16),
            pltpu.VMEM((2, n_y - 1, chunk, half), bf16),
            pltpu.VMEM((2, n_y - 1, chunk, half), bf16),
            pltpu.VMEM((2, chunk, half), f32),
            pltpu.VMEM((2, virt, virt), bf16),
            pltpu.VMEM((rows, virt), f32),
            pltpu.VMEM((virt, LANES), f32),
            pltpu.VMEM((8, virt), f32),
            dma((n_y,)), dma((n_y,)),
            dma((3,)), dma((3,)),
            dma((3,)), dma((3,)),
            dma((3,)), dma((3,)),
            dma((3,)), dma((3,)),
            dma((2, n_y - 1)), dma((2, n_y - 1)),
            dma((2,)), dma((2,)),
            dma((2,)), dma((2,)),
            dma((2, 2, 2)), dma((2, 2, 2)),
            dma((2, 2)), dma((2, 2)),
        ],
        compiler_params=pltpu.CompilerParams(
            collective_id=0, has_side_effects=True, vmem_limit_bytes=60 * 2**20
        ),
    )(
        factor.reshape(rows, virt),
        occ_energy.reshape(-1, LANES),
        vir_energy.reshape(-1, LANES),
        occ_pick,
        vir_pick.reshape(-1, LANES),
    )
    return out.reshape(rows, 1, virt)


def solution(mesh):
    placed = (P("aux", "occ", None), P(), P(), P(), P())
    return jax.shard_map(
        on_device, mesh=mesh, in_specs=placed, out_specs=P("aux", "occ", None), check_vma=False
    )
```

```python
import functools

import jax
import jax.numpy as jnp
from jax import lax
from jax.experimental import pallas as pl
from jax.experimental.pallas import tpu as pltpu
from jax.sharding import PartitionSpec as P

MESH = pl.DeviceIdType.MESH
LANES = 128


def kernel(
    n_y, n_occ, f_ref, oe_ref, ve_ref, op_ref, vp_ref, out_ref,
    fx, ft, jj, jx, sb, rb, acc, tt, g1, vcol, vrow,
    g_s, g_r, z_s, z_r, w_s, w_r, q_s, q_r, s_s, s_r, rs_s, rs_r, ax_s, ax_r, af_s, af_r, a1_s, a1_r, a2_s, a2_r, turn_sem,
):
    rows, virt = f_ref.shape
    half = virt // 2
    chunk = virt // n_y
    sub = chunk // 2
    aux, occ = lax.axis_index("aux"), lax.axis_index("occ")
    h, y = aux // n_y, aux % n_y
    core = occ % 2

    def at_y(step):
        return {"aux": h * n_y + (y + step) % n_y}

    partner = {"aux": (1 - h) * n_y + y}
    sibling = {"occ": occ + 1 - 2 * core}
    ahead = {"occ": (occ + 2) % n_occ}
    behind = {"occ": (occ + n_occ - 2) % n_occ}
    wraps = (occ + 2) % (n_occ // 2) < 2
    ahead_across = {"aux": (1 - h) * n_y + y, "occ": (occ + 2) % n_occ}
    facing = {"occ": (occ + n_occ // 2) % n_occ}
    column = occ // (n_occ // 2) * (n_occ // 2)
    up_column = {"occ": column + (occ + 2) % (n_occ // 2)}
    down_column = {"occ": column + (occ + n_occ // 2 - 2) % (n_occ // 2)}
    behind_across = {"aux": (1 - h) * n_y + y, "occ": (occ + n_occ - 2) % n_occ}

    def send(src, dst, s_sem, r_sem, where):
        return pltpu.make_async_remote_copy(
            src_ref=src, dst_ref=dst, send_sem=s_sem, recv_sem=r_sem,
            device_id=where, device_id_type=MESH,
        )

    def cols(start, size):
        return pl.ds(pl.multiple_of(start, LANES), size)

    mine, other = cols(h * half, half), cols((1 - h) * half, half)

    barrier = pltpu.get_barrier_semaphore()
    peers = [partner, sibling, ahead, behind, ahead_across, behind_across]
    peers = peers + [facing, up_column, down_column] + [at_y(k) for k in range(1, n_y)]
    for peer in peers:
        pl.semaphore_signal(barrier, inc=1, device_id=peer, device_id_type=MESH)
    pl.semaphore_wait(barrier, len(peers))

    def order(k, half_at):
        per_half = n_y // 2
        return (half_at + k // per_half) % 2 * per_half + (y + 1 + k) % per_half

    def gather(k, half_at):
        c = cols(order(k, half_at) * chunk, chunk)
        return send(f_ref.at[:, c], fx.at[:, c], g_s.at[k], g_r.at[k], partner)

    for k in range(n_y // 2):
        gather(k, 1 - h).start()

    @pl.when(core == 1)
    def _():
        for k in range(n_y // 2, n_y):
            gather(k, 1 - h).start()


    upper, lower = pl.ds(rows // 2, rows // 2), pl.ds(0, rows // 2)

    class Ahead:
        def __init__(self, part):
            c = mine if part == 0 else other
            self.direct = send(f_ref.at[lower, c], jj.at[1, lower, c], z_s.at[part], z_r.at[part], ahead)
            self.second = send(f_ref.at[upper, c], jj.at[1, upper, c], w_s.at[part], w_r.at[part], ahead)
            self.detour = send(f_ref.at[upper, c], jj.at[2, upper, c], w_s.at[part], q_r.at[part], facing)
            self.onward = send(jj.at[2, upper, c], jj.at[1, upper, c], q_s.at[part], w_r.at[part], up_column)

        def start(self):
            @pl.when(wraps)
            def _():
                self.detour.start()

            self.direct.start()

            @pl.when(jnp.logical_not(wraps))
            def _():
                self.second.start()

        def hand_on(self):
            @pl.when(wraps)
            def _():
                self.detour.wait_recv()
                self.onward.start()

        def wait_recv(self):
            self.direct.wait_recv()
            self.second.wait_recv()

        def wait_send(self):
            self.direct.wait_send()
            self.second.wait_send()

            @pl.when(wraps)
            def _():
                self.onward.wait_send()

    ahead_parts = (
        Ahead(0),
        send(fx.at[:, mine], jx.at[1], z_s.at[1], z_r.at[1], ahead),
        Ahead(2),
    )
    straight = send(f_ref.at[:, other], jx.at[1], z_s.at[1], z_r.at[1], ahead_across)

    down_parts = (
        send(f_ref.at[:, mine], jj.at[0, :, mine], s_s.at[0], s_r.at[0], sibling),
        send(fx.at[:, mine], jx.at[0], s_s.at[1], s_r.at[1], sibling),
        send(f_ref.at[:, other], jj.at[0, :, other], s_s.at[2], s_r.at[2], sibling),
    )
    up_parts = (
        send(jj.at[1, :, mine], jj.at[0, :, mine], s_s.at[0], s_r.at[0], sibling),
        send(jx.at[1], jx.at[0], s_s.at[1], s_r.at[1], sibling),
        send(jj.at[1, :, other], jj.at[0, :, other], s_s.at[2], s_r.at[2], sibling),
    )
    @pl.when(wraps)
    def _():
        straight.start()

    @pl.when(core == 1)
    def _():
        ahead_parts[0].start()

    @pl.when(core == 0)
    def _():
        down_parts[0].start()

    def turn(src, c, at):
        def body(t, carry):
            start = pl.multiple_of(c * chunk + t * LANES, LANES)
            ft[pl.ds(start, LANES), at * rows : (at + 1) * rows] = src[:, pl.ds(start, LANES)].T
            return carry

        lax.fori_loop(0, chunk // LANES, body, 0)

    def turn_own(k, carry):
        turn(f_ref, order(k, h), 0)
        return carry

    lax.fori_loop(0, n_y, turn_own, 0)

    n_tiles = ve_ref.shape[0]
    lane = lax.broadcasted_iota(jnp.int32, (LANES, LANES), 1)

    def levels(g, carry):
        pick = jnp.broadcast_to(vp_ref[pl.ds(g, 1), :], (LANES, LANES)).T

        def one(m, total):
            energy = jnp.broadcast_to(ve_ref[pl.ds(m, 1), :], (LANES, LANES))
            return total + jnp.where(pick == lane + m * LANES, energy, 0.0)

        total = lax.fori_loop(0, n_tiles, one, jnp.zeros((LANES, LANES), jnp.float32))
        level = jnp.broadcast_to(jnp.sum(total, axis=1, keepdims=True), (LANES, LANES))
        start = pl.multiple_of(g * LANES, LANES)
        vcol[pl.ds(start, LANES), :] = level
        vrow[:, pl.ds(start, LANES)] = level.T[:8]
        return carry

    lax.fori_loop(0, virt // LANES, levels, 0)

    spot = lax.broadcasted_iota(jnp.int32, oe_ref.shape, 0) * LANES
    spot = spot + lax.broadcasted_iota(jnp.int32, oe_ref.shape, 1)

    def occ_level(orbital):
        found = jnp.where(spot == op_ref[orbital], oe_ref[...], 0.0)
        return jnp.sum(jnp.sum(found, axis=1, keepdims=True), axis=0, keepdims=True)

    def own_chunk(k):
        return order(k, h)

    def arrived(k):
        gather(k, h).wait_recv()
        turn(fx, own_chunk(k), 1)

    for k in range(n_y // 2):
        gather(k, h).wait_recv()

    @pl.when(jnp.logical_not(wraps))
    def _():
        ahead_parts[1].start()

    @pl.when(core == 0)
    def _():
        down_parts[1].start()
        down_parts[2].start()

        ahead_parts[0].start()

    @pl.when(core == 1)
    def _():
        ahead_parts[0].hand_on()

    for k in range(n_y // 2):
        turn(fx, own_chunk(k), 1)

    width = 256

    def partial_integrals(s, c):
        r = (c + n_y - y) % n_y
        a_rows = pl.ds(pl.multiple_of(c * chunk, chunk), chunk)

        def body(t, carry):
            start = pl.multiple_of(t * width, width)
            b_cols = cols(h * half + start, width)
            total = jnp.dot(
                ft[a_rows, :rows], jj[s, :, b_cols], preferred_element_type=jnp.float32
            )
            total = total + jnp.dot(
                ft[a_rows, rows:], jx[s, :, pl.ds(start, width)],
                preferred_element_type=jnp.float32,
            )

            @pl.when(r == 0)
            def _():
                acc[s, :, pl.ds(start, width)] = total

            @pl.when(r != 0)
            def _():
                sb[s, r - 1, :, pl.ds(start, width)] = total.astype(jnp.bfloat16)

            return carry

        lax.fori_loop(0, half // width, body, 0)

        @pl.when(r != 0)
        def _():
            send(
                sb.at[s, r - 1], rb.at[s, n_y - 1 - r], rs_s.at[s, r - 1],
                rs_r.at[s, n_y - 1 - r], {"aux": h * n_y + c},
            ).start()

    my_rows = pl.ds(pl.multiple_of(y * chunk, chunk), chunk)

    def finish(s):
        for k in range(n_y - 1):
            send(
                sb.at[s, k], rb.at[s, k], rs_s.at[s, k], rs_r.at[s, k], at_y(1)
            ).wait_recv()
        level = occ_level(occ) + occ_level((occ + n_occ - 1 - s) % n_occ)

        def body(t, carry):
            at = pl.ds(pl.multiple_of(t * 64, 64), 64)
            left = level - vcol[pl.ds(pl.multiple_of(y * chunk + t * 64, 64), 64), :]

            def inner(u, carry):
                c = pl.ds(pl.multiple_of(u * LANES, LANES), LANES)
                there = cols(h * half + u * LANES, LANES)
                total = acc[s, at, c]
                for k in range(n_y - 1):
                    total = total + rb[s, k, at, c].astype(jnp.float32)
                divisor = left - vrow[:1, there]
                tt[s, pl.ds(pl.multiple_of(y * chunk + t * 64, 64), 64), there] = (
                    total / divisor
                ).astype(jnp.bfloat16)
                return carry

            return lax.fori_loop(0, half // LANES, inner, carry)

        lax.fori_loop(0, chunk // 64, body, 0)

    def block(s, y_at, which, lo=0, size=None):
        start = pl.multiple_of((y + y_at + n_y) % n_y * chunk + lo, sub)
        return tt.at[s, pl.ds(start, size or chunk), mine if which == 0 else other]

    def across(s):
        part = block(s, 0, 0)
        return send(part, part, ax_s.at[s], ax_r.at[s], partner)

    def across_far(s):
        part = block(s, 2, 0)
        return send(part, part, af_s.at[s], af_r.at[s], partner)

    def along(s, which, way):
        part = block(s, 0, which)
        return send(part, part, a1_s.at[s, which, way], a1_r.at[s, which, way], at_y(1 if way == 0 else n_y - 1))

    def onward(s, way):
        part = block(s, -1 if way == 0 else 1, 0, 0 if way == 0 else sub, sub)
        return send(part, part, a2_s.at[s, way], a2_r.at[s, way], at_y(1 if way == 0 else n_y - 1))

    def spread_own(s):
        across(s).start()
        along(s, 0, 0).start()
        along(s, 0, 1).start()

    def spread_partner(s):
        across(s).wait_recv()
        along(s, 1, 0).start()
        along(s, 1, 1).start()

    def forward(s):
        for way in (0, 1):
            along(s, 0, way).wait_recv()
            onward(s, way).start()

    def spread_far(s):
        for way in (0, 1):
            onward(s, way).wait_recv()
        across_far(s).start()

    def gathered(s):
        for way in (0, 1):
            along(s, 1, way).wait_recv()
        across_far(s).wait_recv()

    first, second = 0, 1

    def relay(part):
        @pl.when(core == 1)
        def _():
            ahead_parts[part].wait_recv()
            up_parts[part].start()

    def given(part):
        down_parts[part].wait_recv()

    @pl.when(core == 1)
    def _():
        given(0)
        given(1)
        for k in range(n_y // 2):
            partial_integrals(first, own_chunk(k))

    @pl.when(core == 0)
    def _():
        pl.semaphore_wait(turn_sem, 1)
        for k in range(n_y // 2, n_y):
            gather(k, 1 - h).start()

    for k in range(n_y // 2, n_y):
        arrived(k)
        if k == n_y - 1:
            @pl.when(core == 1)
            def _():
                pl.semaphore_signal(turn_sem, inc=1, device_id=sibling, device_id_type=MESH)

        @pl.when(core == 1)
        def _():
            partial_integrals(first, own_chunk(k))

    @pl.when(core == 0)
    def _():
        ahead_parts[0].hand_on()

    def chunks(s):
        def body(k, carry):
            partial_integrals(s, (y + k) % n_y)
            return carry

        lax.fori_loop(1, n_y + 1, body, 0)

    @pl.when(core == 0)
    def _():
        given(0)
        given(1)
        chunks(first)

    relay(0)
    relay(1)
    finish(first)
    spread_own(first)

    @pl.when(core == 1)
    def _():
        chunks(second)

    @pl.when(core == 0)
    def _():
        ahead_parts[0].wait_recv()
        ahead_parts[1].wait_recv()
        chunks(second)

    ahead_parts[2].start()
    forward(first)
    spread_partner(first)
    ahead_parts[2].hand_on()
    finish(second)
    spread_own(second)
    spread_far(first)
    relay(2)
    forward(second)
    spread_partner(second)
    gathered(first)
    given(2)

    def density(s, t):
        a_rows = pl.ds(pl.multiple_of(t * width, width), width)
        return lax.dot_general(
            jj[s], tt[s, a_rows, :], (((1,), (1,)), ((), ())), preferred_element_type=jnp.float32
        )

    def first_density(t, carry):
        g1[:, pl.ds(pl.multiple_of(t * width, width), width)] = density(first, t)
        return carry

    lax.fori_loop(0, virt // (2 * width), first_density, 0)
    spread_far(second)
    lax.fori_loop(virt // (2 * width), virt // width, first_density, 0)

    @pl.when(core == 0)
    def _():
        ahead_parts[2].wait_recv()

    gathered(second)
    per_row = virt // LANES

    def last_density(t, carry):
        total = density(second, t) + g1[:, pl.ds(pl.multiple_of(t * width, width), width)]
        for u in range(width // LANES):
            out_ref[pl.ds(t * (width // LANES) + u, rows, stride=per_row), :] = total[
                :, u * LANES : (u + 1) * LANES
            ]
        return carry

    lax.fori_loop(0, virt // width, last_density, 0)

    for k in range(n_y):
        gather(k, 1 - h).wait_send()
    for part in range(3):
        ahead_parts[part].wait_send()
        down_parts[part].wait_send()
    for s in (0, 1):
        for k in range(n_y - 1):
            send(
                sb.at[s, k], rb.at[s, k], rs_s.at[s, k], rs_r.at[s, k], at_y(1)
            ).wait_send()
        across(s).wait_send()
        across_far(s).wait_send()
        for way in (0, 1):
            along(s, 0, way).wait_send()
            along(s, 1, way).wait_send()
            onward(s, way).wait_send()


def on_device(factor, occ_energy, vir_energy, occ_pick, vir_pick):
    n_aux, n_occ = lax.axis_size("aux"), lax.axis_size("occ")
    n_y = n_aux // 2
    rows, _, virt = factor.shape
    half, chunk = virt // 2, virt // n_y
    bf16, f32 = jnp.bfloat16, jnp.float32
    dma = pltpu.SemaphoreType.DMA
    vmem = pl.BlockSpec(memory_space=pltpu.VMEM)
    out = pl.pallas_call(
        functools.partial(kernel, n_y, n_occ),
        out_shape=jax.ShapeDtypeStruct((rows * virt // LANES, LANES), f32),
        in_specs=[vmem, vmem, vmem, pl.BlockSpec(memory_space=pltpu.SMEM), vmem],
        out_specs=vmem,
        scratch_shapes=[
            pltpu.VMEM((rows, virt), bf16),
            pltpu.VMEM((virt, 2 * rows), bf16),
            pltpu.VMEM((3, rows, virt), bf16),
            pltpu.VMEM((2, rows, half), bf16),
            pltpu.VMEM((2, n_y - 1, chunk, half), bf16),
            pltpu.VMEM((2, n_y - 1, chunk, half), bf16),
            pltpu.VMEM((2, chunk, half), f32),
            pltpu.VMEM((2, virt, virt), bf16),
            pltpu.VMEM((rows, virt), f32),
            pltpu.VMEM((virt, LANES), f32),
            pltpu.VMEM((8, virt), f32),
            dma((n_y,)), dma((n_y,)),
            dma((3,)), dma((3,)),
            dma((3,)), dma((3,)),
            dma((3,)), dma((3,)),
            dma((3,)), dma((3,)),
            dma((2, n_y - 1)), dma((2, n_y - 1)),
            dma((2,)), dma((2,)),
            dma((2,)), dma((2,)),
            dma((2, 2, 2)), dma((2, 2, 2)),
            dma((2, 2)), dma((2, 2)),
            pltpu.SemaphoreType.REGULAR,
        ],
        compiler_params=pltpu.CompilerParams(
            collective_id=0, has_side_effects=True, vmem_limit_bytes=60 * 2**20
        ),
    )(
        factor.reshape(rows, virt),
        occ_energy.reshape(-1, LANES),
        vir_energy.reshape(-1, LANES),
        occ_pick,
        vir_pick.reshape(-1, LANES),
    )
    return out.reshape(rows, 1, virt)


def solution(mesh):
    placed = (P("aux", "occ", None), P(), P(), P(), P())
    return jax.shard_map(
        on_device, mesh=mesh, in_specs=placed, out_specs=P("aux", "occ", None), check_vma=False
    )
```

```python
import functools

import jax
import jax.numpy as jnp
from jax import lax
from jax.experimental import pallas as pl
from jax.experimental.pallas import tpu as pltpu
from jax.sharding import PartitionSpec as P

MESH = pl.DeviceIdType.MESH
LANES = 128


def kernel(
    n_y, n_occ, f_ref, oe_ref, ve_ref, op_ref, vp_ref, out_ref,
    fx, ft, jj, jx, sb, rb, acc, tt, g1, vcol, vrow,
    g_s, g_r, z_s, z_r, w_s, w_r, q_s, q_r, s_s, s_r, rs_s, rs_r, ax_s, ax_r, af_s, af_r, a1_s, a1_r, a2_s, a2_r, turn_sem,
):
    rows, virt = f_ref.shape
    half = virt // 2
    chunk = virt // n_y
    sub = chunk // 2
    aux, occ = lax.axis_index("aux"), lax.axis_index("occ")
    h, y = aux // n_y, aux % n_y
    core = occ % 2

    def at_y(step):
        return {"aux": h * n_y + (y + step) % n_y}

    partner = {"aux": (1 - h) * n_y + y}
    sibling = {"occ": occ + 1 - 2 * core}
    ahead = {"occ": (occ + 2) % n_occ}
    behind = {"occ": (occ + n_occ - 2) % n_occ}
    wraps = (occ + 2) % (n_occ // 2) < 2
    ahead_across = {"aux": (1 - h) * n_y + y, "occ": (occ + 2) % n_occ}
    facing = {"occ": (occ + n_occ // 2) % n_occ}
    column = occ // (n_occ // 2) * (n_occ // 2)
    up_column = {"occ": column + (occ + 2) % (n_occ // 2)}
    down_column = {"occ": column + (occ + n_occ // 2 - 2) % (n_occ // 2)}
    behind_across = {"aux": (1 - h) * n_y + y, "occ": (occ + n_occ - 2) % n_occ}

    def send(src, dst, s_sem, r_sem, where):
        return pltpu.make_async_remote_copy(
            src_ref=src, dst_ref=dst, send_sem=s_sem, recv_sem=r_sem,
            device_id=where, device_id_type=MESH,
        )

    def cols(start, size):
        return pl.ds(pl.multiple_of(start, LANES), size)

    mine, other = cols(h * half, half), cols((1 - h) * half, half)

    barrier = pltpu.get_barrier_semaphore()
    peers = [partner, sibling, ahead, behind, ahead_across, behind_across]
    peers = peers + [facing, up_column, down_column] + [at_y(k) for k in range(1, n_y)]
    for peer in peers:
        pl.semaphore_signal(barrier, inc=1, device_id=peer, device_id_type=MESH)
    pl.semaphore_wait(barrier, len(peers))

    def order(k, half_at):
        per_half = n_y // 2
        return (half_at + k // per_half) % 2 * per_half + (y + 1 + k) % per_half

    def gather(k, half_at):
        c = cols(order(k, half_at) * chunk, chunk)
        return send(f_ref.at[:, c], fx.at[:, c], g_s.at[k], g_r.at[k], partner)

    for k in range(n_y // 2):
        gather(k, 1 - h).start()

    @pl.when(core == 1)
    def _():
        for k in range(n_y // 2, n_y):
            gather(k, 1 - h).start()


    upper, lower = pl.ds(rows // 2, rows // 2), pl.ds(0, rows // 2)

    class Ahead:
        def __init__(self, part):
            c = mine if part == 0 else other
            self.direct = send(f_ref.at[lower, c], jj.at[1, lower, c], z_s.at[part], z_r.at[part], ahead)
            self.second = send(f_ref.at[upper, c], jj.at[1, upper, c], w_s.at[part], w_r.at[part], ahead)
            self.detour = send(f_ref.at[upper, c], jj.at[2, upper, c], w_s.at[part], q_r.at[part], facing)
            self.onward = send(jj.at[2, upper, c], jj.at[1, upper, c], q_s.at[part], w_r.at[part], up_column)

        def start(self):
            @pl.when(wraps)
            def _():
                self.detour.start()

            self.direct.start()

            @pl.when(jnp.logical_not(wraps))
            def _():
                self.second.start()

        def hand_on(self):
            @pl.when(wraps)
            def _():
                self.detour.wait_recv()
                self.onward.start()

        def wait_recv(self):
            self.direct.wait_recv()
            self.second.wait_recv()

        def wait_send(self):
            self.direct.wait_send()
            self.second.wait_send()

            @pl.when(wraps)
            def _():
                self.onward.wait_send()

    ahead_parts = (
        Ahead(0),
        send(fx.at[:, mine], jx.at[1], z_s.at[1], z_r.at[1], ahead),
        Ahead(2),
    )
    straight = send(f_ref.at[:, other], jx.at[1], z_s.at[1], z_r.at[1], ahead_across)

    down_parts = (
        send(f_ref.at[:, mine], jj.at[0, :, mine], s_s.at[0], s_r.at[0], sibling),
        send(fx.at[:, mine], jx.at[0], s_s.at[1], s_r.at[1], sibling),
        send(f_ref.at[:, other], jj.at[0, :, other], s_s.at[2], s_r.at[2], sibling),
    )
    up_parts = (
        send(jj.at[1, :, mine], jj.at[0, :, mine], s_s.at[0], s_r.at[0], sibling),
        send(jx.at[1], jx.at[0], s_s.at[1], s_r.at[1], sibling),
        send(jj.at[1, :, other], jj.at[0, :, other], s_s.at[2], s_r.at[2], sibling),
    )
    @pl.when(wraps)
    def _():
        straight.start()

    @pl.when(core == 1)
    def _():
        ahead_parts[0].start()

    @pl.when(core == 0)
    def _():
        down_parts[0].start()

    def turn(src, c, at):
        def body(t, carry):
            start = pl.multiple_of(c * chunk + t * LANES, LANES)
            ft[pl.ds(start, LANES), at * rows : (at + 1) * rows] = src[:, pl.ds(start, LANES)].T
            return carry

        lax.fori_loop(0, chunk // LANES, body, 0)

    def turn_own(k, carry):
        turn(f_ref, order(k, h), 0)
        return carry

    lax.fori_loop(0, n_y, turn_own, 0)

    n_tiles = ve_ref.shape[0]
    lane = lax.broadcasted_iota(jnp.int32, (LANES, LANES), 1)

    def levels(g, carry):
        pick = jnp.broadcast_to(vp_ref[pl.ds(g, 1), :], (LANES, LANES)).T

        def one(m, total):
            energy = jnp.broadcast_to(ve_ref[pl.ds(m, 1), :], (LANES, LANES))
            return total + jnp.where(pick == lane + m * LANES, energy, 0.0)

        total = lax.fori_loop(0, n_tiles, one, jnp.zeros((LANES, LANES), jnp.float32))
        level = jnp.broadcast_to(jnp.sum(total, axis=1, keepdims=True), (LANES, LANES))
        start = pl.multiple_of(g * LANES, LANES)
        vcol[pl.ds(start, LANES), :] = level
        vrow[:, pl.ds(start, LANES)] = level.T[:8]
        return carry

    lax.fori_loop(0, virt // LANES, levels, 0)

    spot = lax.broadcasted_iota(jnp.int32, oe_ref.shape, 0) * LANES
    spot = spot + lax.broadcasted_iota(jnp.int32, oe_ref.shape, 1)

    def occ_level(orbital):
        found = jnp.where(spot == op_ref[orbital], oe_ref[...], 0.0)
        return jnp.sum(jnp.sum(found, axis=1, keepdims=True), axis=0, keepdims=True)

    def own_chunk(k):
        return order(k, h)

    def arrived(k):
        gather(k, h).wait_recv()
        turn(fx, own_chunk(k), 1)

    for k in range(n_y // 2):
        gather(k, h).wait_recv()

    @pl.when(jnp.logical_not(wraps))
    def _():
        ahead_parts[1].start()

    @pl.when(core == 0)
    def _():
        down_parts[1].start()
        down_parts[2].start()

        @pl.when(jnp.logical_not(wraps))
        def _():
            ahead_parts[0].start()

    @pl.when(core == 1)
    def _():
        ahead_parts[0].hand_on()

    for k in range(n_y // 2):
        turn(fx, own_chunk(k), 1)

    width = 256

    def partial_integrals(s, c):
        r = (c + n_y - y) % n_y
        a_rows = pl.ds(pl.multiple_of(c * chunk, chunk), chunk)

        def body(t, carry):
            start = pl.multiple_of(t * width, width)
            b_cols = cols(h * half + start, width)
            total = jnp.dot(
                ft[a_rows, :rows], jj[s, :, b_cols], preferred_element_type=jnp.float32
            )
            total = total + jnp.dot(
                ft[a_rows, rows:], jx[s, :, pl.ds(start, width)],
                preferred_element_type=jnp.float32,
            )

            @pl.when(r == 0)
            def _():
                acc[s, :, pl.ds(start, width)] = total

            @pl.when(r != 0)
            def _():
                sb[s, r - 1, :, pl.ds(start, width)] = total.astype(jnp.bfloat16)

            return carry

        lax.fori_loop(0, half // width, body, 0)

        @pl.when(r != 0)
        def _():
            send(
                sb.at[s, r - 1], rb.at[s, n_y - 1 - r], rs_s.at[s, r - 1],
                rs_r.at[s, n_y - 1 - r], {"aux": h * n_y + c},
            ).start()

    my_rows = pl.ds(pl.multiple_of(y * chunk, chunk), chunk)

    def finish(s):
        for k in range(n_y - 1):
            send(
                sb.at[s, k], rb.at[s, k], rs_s.at[s, k], rs_r.at[s, k], at_y(1)
            ).wait_recv()
        level = occ_level(occ) + occ_level((occ + n_occ - 1 - s) % n_occ)

        def body(t, carry):
            at = pl.ds(pl.multiple_of(t * 64, 64), 64)
            left = level - vcol[pl.ds(pl.multiple_of(y * chunk + t * 64, 64), 64), :]

            def inner(u, carry):
                c = pl.ds(pl.multiple_of(u * LANES, LANES), LANES)
                there = cols(h * half + u * LANES, LANES)
                total = acc[s, at, c]
                for k in range(n_y - 1):
                    total = total + rb[s, k, at, c].astype(jnp.float32)
                divisor = left - vrow[:1, there]
                tt[s, pl.ds(pl.multiple_of(y * chunk + t * 64, 64), 64), there] = (
                    total / divisor
                ).astype(jnp.bfloat16)
                return carry

            return lax.fori_loop(0, half // LANES, inner, carry)

        lax.fori_loop(0, chunk // 64, body, 0)

    def block(s, y_at, which, lo=0, size=None):
        start = pl.multiple_of((y + y_at + n_y) % n_y * chunk + lo, sub)
        return tt.at[s, pl.ds(start, size or chunk), mine if which == 0 else other]

    def across(s):
        part = block(s, 0, 0)
        return send(part, part, ax_s.at[s], ax_r.at[s], partner)

    def across_far(s):
        part = block(s, 2, 0)
        return send(part, part, af_s.at[s], af_r.at[s], partner)

    def along(s, which, way):
        part = block(s, 0, which)
        return send(part, part, a1_s.at[s, which, way], a1_r.at[s, which, way], at_y(1 if way == 0 else n_y - 1))

    def onward(s, way):
        part = block(s, -1 if way == 0 else 1, 0, 0 if way == 0 else sub, sub)
        return send(part, part, a2_s.at[s, way], a2_r.at[s, way], at_y(1 if way == 0 else n_y - 1))

    def spread_own(s):
        across(s).start()
        along(s, 0, 0).start()
        along(s, 0, 1).start()

    def spread_partner(s):
        across(s).wait_recv()
        along(s, 1, 0).start()
        along(s, 1, 1).start()

    def forward(s):
        for way in (0, 1):
            along(s, 0, way).wait_recv()
            onward(s, way).start()

    def spread_far(s):
        for way in (0, 1):
            onward(s, way).wait_recv()
        across_far(s).start()

    def gathered(s):
        for way in (0, 1):
            along(s, 1, way).wait_recv()
        across_far(s).wait_recv()

    first, second = 0, 1

    def relay(part):
        @pl.when(core == 1)
        def _():
            ahead_parts[part].wait_recv()
            up_parts[part].start()

    def given(part):
        down_parts[part].wait_recv()

    @pl.when(core == 1)
    def _():
        given(0)
        given(1)
        for k in range(n_y // 2):
            partial_integrals(first, own_chunk(k))

    @pl.when(core == 0)
    def _():
        pl.semaphore_wait(turn_sem, 1)

        @pl.when(wraps)
        def _():
            ahead_parts[0].start()

        for k in range(n_y // 2, n_y):
            gather(k, 1 - h).start()

    for k in range(n_y // 2, n_y):
        arrived(k)
        if k == n_y - 1:
            @pl.when(core == 1)
            def _():
                pl.semaphore_signal(turn_sem, inc=1, device_id=sibling, device_id_type=MESH)

        @pl.when(core == 1)
        def _():
            partial_integrals(first, own_chunk(k))

    @pl.when(core == 0)
    def _():
        ahead_parts[0].hand_on()

    def chunks(s):
        def body(k, carry):
            partial_integrals(s, (y + k) % n_y)
            return carry

        lax.fori_loop(1, n_y + 1, body, 0)

    @pl.when(core == 0)
    def _():
        given(0)
        given(1)
        chunks(first)

    relay(0)
    relay(1)
    finish(first)
    spread_own(first)

    @pl.when(core == 1)
    def _():
        chunks(second)

    @pl.when(core == 0)
    def _():
        ahead_parts[0].wait_recv()
        ahead_parts[1].wait_recv()
        chunks(second)

    ahead_parts[2].start()
    spread_partner(first)
    forward(first)
    ahead_parts[2].hand_on()
    finish(second)
    spread_own(second)
    spread_far(first)
    relay(2)
    forward(second)
    spread_partner(second)
    gathered(first)
    given(2)

    def density(s, t):
        a_rows = pl.ds(pl.multiple_of(t * width, width), width)
        return lax.dot_general(
            jj[s], tt[s, a_rows, :], (((1,), (1,)), ((), ())), preferred_element_type=jnp.float32
        )

    def first_density(t, carry):
        g1[:, pl.ds(pl.multiple_of(t * width, width), width)] = density(first, t)
        return carry

    lax.fori_loop(0, virt // (2 * width), first_density, 0)
    spread_far(second)
    lax.fori_loop(virt // (2 * width), virt // width, first_density, 0)

    @pl.when(core == 0)
    def _():
        ahead_parts[2].wait_recv()

    gathered(second)
    per_row = virt // LANES

    def last_density(t, carry):
        total = density(second, t) + g1[:, pl.ds(pl.multiple_of(t * width, width), width)]
        for u in range(width // LANES):
            out_ref[pl.ds(t * (width // LANES) + u, rows, stride=per_row), :] = total[
                :, u * LANES : (u + 1) * LANES
            ]
        return carry

    lax.fori_loop(0, virt // width, last_density, 0)

    for k in range(n_y):
        gather(k, 1 - h).wait_send()
    for part in range(3):
        ahead_parts[part].wait_send()
        down_parts[part].wait_send()
    for s in (0, 1):
        for k in range(n_y - 1):
            send(
                sb.at[s, k], rb.at[s, k], rs_s.at[s, k], rs_r.at[s, k], at_y(1)
            ).wait_send()
        across(s).wait_send()
        across_far(s).wait_send()
        for way in (0, 1):
            along(s, 0, way).wait_send()
            along(s, 1, way).wait_send()
            onward(s, way).wait_send()


def hand_over(from_ref, to_ref):
    to_ref[...] = from_ref[...]


def on_device(factor, occ_energy, vir_energy, occ_pick, vir_pick):
    n_aux, n_occ = lax.axis_size("aux"), lax.axis_size("occ")
    n_y = n_aux // 2
    rows, _, virt = factor.shape
    half, chunk = virt // 2, virt // n_y
    bf16, f32 = jnp.bfloat16, jnp.float32
    dma = pltpu.SemaphoreType.DMA
    vmem = pl.BlockSpec(memory_space=pltpu.VMEM)
    out = pl.pallas_call(
        functools.partial(kernel, n_y, n_occ),
        out_shape=jax.ShapeDtypeStruct((rows * virt // LANES, LANES), f32),
        in_specs=[vmem, vmem, vmem, pl.BlockSpec(memory_space=pltpu.SMEM), vmem],
        out_specs=vmem,
        scratch_shapes=[
            pltpu.VMEM((rows, virt), bf16),
            pltpu.VMEM((virt, 2 * rows), bf16),
            pltpu.VMEM((3, rows, virt), bf16),
            pltpu.VMEM((2, rows, half), bf16),
            pltpu.VMEM((2, n_y - 1, chunk, half), bf16),
            pltpu.VMEM((2, n_y - 1, chunk, half), bf16),
            pltpu.VMEM((2, chunk, half), f32),
            pltpu.VMEM((2, virt, virt), bf16),
            pltpu.VMEM((rows, virt), f32),
            pltpu.VMEM((virt, LANES), f32),
            pltpu.VMEM((8, virt), f32),
            dma((n_y,)), dma((n_y,)),
            dma((3,)), dma((3,)),
            dma((3,)), dma((3,)),
            dma((3,)), dma((3,)),
            dma((3,)), dma((3,)),
            dma((2, n_y - 1)), dma((2, n_y - 1)),
            dma((2,)), dma((2,)),
            dma((2,)), dma((2,)),
            dma((2, 2, 2)), dma((2, 2, 2)),
            dma((2, 2)), dma((2, 2)),
            pltpu.SemaphoreType.REGULAR,
        ],
        compiler_params=pltpu.CompilerParams(
            collective_id=0, has_side_effects=True, vmem_limit_bytes=60 * 2**20
        ),
    )(
        factor.reshape(rows, virt),
        occ_energy.reshape(-1, LANES),
        vir_energy.reshape(-1, LANES),
        occ_pick,
        vir_pick.reshape(-1, LANES),
    )
    out = pl.pallas_call(
        hand_over,
        out_shape=jax.ShapeDtypeStruct(out.shape, f32),
        grid=(4,),
        in_specs=[pl.BlockSpec((out.shape[0] // 4, LANES), lambda i: (i, 0))],
        out_specs=pl.BlockSpec((out.shape[0] // 4, LANES), lambda i: (i, 0)),
    )(out)
    return out.reshape(rows, 1, virt)


def solution(mesh):
    placed = (P("aux", "occ", None), P(), P(), P(), P())
    return jax.shard_map(
        on_device, mesh=mesh, in_specs=placed, out_specs=P("aux", "occ", None), check_vma=False
    )
```

```python
import functools

import jax
import jax.numpy as jnp
from jax import lax
from jax.experimental import pallas as pl
from jax.experimental.pallas import tpu as pltpu
from jax.sharding import PartitionSpec as P

MESH = pl.DeviceIdType.MESH
LANES = 128


def kernel(
    n_y, n_occ, f_ref, oe_ref, ve_ref, op_ref, vp_ref, out_ref,
    fx, ft, jj, jx, sb, rb, acc, tt, g1, vcol, vrow,
    g_s, g_r, z_s, z_r, w_s, w_r, q_s, q_r, s_s, s_r, rs_s, rs_r, ax_s, ax_r, af_s, af_r, a1_s, a1_r, a2_s, a2_r, turn_sem,
):
    rows, virt = f_ref.shape
    half = virt // 2
    chunk = virt // n_y
    sub = chunk // 2
    aux, occ = lax.axis_index("aux"), lax.axis_index("occ")
    h, y = aux // n_y, aux % n_y
    core = occ % 2

    def at_y(step):
        return {"aux": h * n_y + (y + step) % n_y}

    partner = {"aux": (1 - h) * n_y + y}
    sibling = {"occ": occ + 1 - 2 * core}
    ahead = {"occ": (occ + 2) % n_occ}
    behind = {"occ": (occ + n_occ - 2) % n_occ}
    wraps = (occ + 2) % (n_occ // 2) < 2
    ahead_across = {"aux": (1 - h) * n_y + y, "occ": (occ + 2) % n_occ}
    facing = {"occ": (occ + n_occ // 2) % n_occ}
    column = occ // (n_occ // 2) * (n_occ // 2)
    up_column = {"occ": column + (occ + 2) % (n_occ // 2)}
    down_column = {"occ": column + (occ + n_occ // 2 - 2) % (n_occ // 2)}
    behind_across = {"aux": (1 - h) * n_y + y, "occ": (occ + n_occ - 2) % n_occ}

    def send(src, dst, s_sem, r_sem, where):
        return pltpu.make_async_remote_copy(
            src_ref=src, dst_ref=dst, send_sem=s_sem, recv_sem=r_sem,
            device_id=where, device_id_type=MESH,
        )

    def cols(start, size):
        return pl.ds(pl.multiple_of(start, LANES), size)

    mine, other = cols(h * half, half), cols((1 - h) * half, half)

    barrier = pltpu.get_barrier_semaphore()
    peers = [partner, sibling, ahead, behind, ahead_across, behind_across]
    peers = peers + [facing, up_column, down_column] + [at_y(k) for k in range(1, n_y)]
    for peer in peers:
        pl.semaphore_signal(barrier, inc=1, device_id=peer, device_id_type=MESH)
    pl.semaphore_wait(barrier, len(peers))

    def order(k, half_at):
        per_half = n_y // 2
        return (half_at + k // per_half) % 2 * per_half + (y + 1 + k) % per_half

    def gather(k, half_at):
        c = cols(order(k, half_at) * chunk, chunk)
        return send(f_ref.at[:, c], fx.at[:, c], g_s.at[k], g_r.at[k], partner)

    for k in range(n_y // 2):
        gather(k, 1 - h).start()

    @pl.when(core == 1)
    def _():
        for k in range(n_y // 2, n_y):
            gather(k, 1 - h).start()


    upper, lower = pl.ds(rows // 2, rows // 2), pl.ds(0, rows // 2)

    class Ahead:
        def __init__(self, part):
            c = mine if part == 0 else other
            self.direct = send(f_ref.at[lower, c], jj.at[1, lower, c], z_s.at[part], z_r.at[part], ahead)
            self.second = send(f_ref.at[upper, c], jj.at[1, upper, c], w_s.at[part], w_r.at[part], ahead)
            self.detour = send(f_ref.at[upper, c], jj.at[2, upper, c], w_s.at[part], q_r.at[part], facing)
            self.onward = send(jj.at[2, upper, c], jj.at[1, upper, c], q_s.at[part], w_r.at[part], up_column)

        def start(self):
            @pl.when(wraps)
            def _():
                self.detour.start()

            self.direct.start()

            @pl.when(jnp.logical_not(wraps))
            def _():
                self.second.start()

        def hand_on(self):
            @pl.when(wraps)
            def _():
                self.detour.wait_recv()
                self.onward.start()

        def wait_recv(self):
            self.direct.wait_recv()
            self.second.wait_recv()

        def wait_send(self):
            self.direct.wait_send()
            self.second.wait_send()

            @pl.when(wraps)
            def _():
                self.onward.wait_send()

    ahead_parts = (
        Ahead(0),
        send(fx.at[:, mine], jx.at[1], z_s.at[1], z_r.at[1], ahead),
        Ahead(2),
    )
    straight = send(f_ref.at[:, other], jx.at[1], z_s.at[1], z_r.at[1], ahead_across)

    down_parts = (
        send(f_ref.at[:, mine], jj.at[0, :, mine], s_s.at[0], s_r.at[0], sibling),
        send(fx.at[:, mine], jx.at[0], s_s.at[1], s_r.at[1], sibling),
        send(f_ref.at[:, other], jj.at[0, :, other], s_s.at[2], s_r.at[2], sibling),
    )
    up_parts = (
        send(jj.at[1, :, mine], jj.at[0, :, mine], s_s.at[0], s_r.at[0], sibling),
        send(jx.at[1], jx.at[0], s_s.at[1], s_r.at[1], sibling),
        send(jj.at[1, :, other], jj.at[0, :, other], s_s.at[2], s_r.at[2], sibling),
    )
    @pl.when(wraps)
    def _():
        straight.start()

    @pl.when(core == 1)
    def _():
        ahead_parts[0].start()

    @pl.when(core == 0)
    def _():
        down_parts[0].start()

    def turn(src, c, at):
        def body(t, carry):
            start = pl.multiple_of(c * chunk + t * LANES, LANES)
            ft[pl.ds(start, LANES), at * rows : (at + 1) * rows] = src[:, pl.ds(start, LANES)].T
            return carry

        lax.fori_loop(0, chunk // LANES, body, 0)

    def turn_own(k, carry):
        turn(f_ref, order(k, h), 0)
        return carry

    lax.fori_loop(0, n_y, turn_own, 0)

    n_tiles = ve_ref.shape[0]
    lane = lax.broadcasted_iota(jnp.int32, (LANES, LANES), 1)

    def levels(g, carry):
        pick = jnp.broadcast_to(vp_ref[pl.ds(g, 1), :], (LANES, LANES)).T

        def one(m, total):
            energy = jnp.broadcast_to(ve_ref[pl.ds(m, 1), :], (LANES, LANES))
            return total + jnp.where(pick == lane + m * LANES, energy, 0.0)

        total = lax.fori_loop(0, n_tiles, one, jnp.zeros((LANES, LANES), jnp.float32))
        level = jnp.broadcast_to(jnp.sum(total, axis=1, keepdims=True), (LANES, LANES))
        start = pl.multiple_of(g * LANES, LANES)
        vcol[pl.ds(start, LANES), :] = level
        vrow[:, pl.ds(start, LANES)] = level.T[:8]
        return carry

    lax.fori_loop(0, virt // LANES, levels, 0)

    spot = lax.broadcasted_iota(jnp.int32, oe_ref.shape, 0) * LANES
    spot = spot + lax.broadcasted_iota(jnp.int32, oe_ref.shape, 1)

    def occ_level(orbital):
        found = jnp.where(spot == op_ref[orbital], oe_ref[...], 0.0)
        return jnp.sum(jnp.sum(found, axis=1, keepdims=True), axis=0, keepdims=True)

    def own_chunk(k):
        return order(k, h)

    def arrived(k):
        gather(k, h).wait_recv()
        turn(fx, own_chunk(k), 1)

    for k in range(n_y // 2):
        gather(k, h).wait_recv()

    @pl.when(jnp.logical_not(wraps))
    def _():
        ahead_parts[1].start()

    @pl.when(core == 0)
    def _():
        down_parts[1].start()
        down_parts[2].start()

        @pl.when(jnp.logical_not(wraps))
        def _():
            ahead_parts[0].start()

    @pl.when(core == 1)
    def _():
        ahead_parts[0].hand_on()

    for k in range(n_y // 2):
        turn(fx, own_chunk(k), 1)

    width = 256

    def partial_integrals(s, c):
        r = (c + n_y - y) % n_y
        a_rows = pl.ds(pl.multiple_of(c * chunk, chunk), chunk)

        def body(t, carry):
            start = pl.multiple_of(t * width, width)
            b_cols = cols(h * half + start, width)
            total = jnp.dot(
                ft[a_rows, :rows], jj[s, :, b_cols], preferred_element_type=jnp.float32
            )
            total = total + jnp.dot(
                ft[a_rows, rows:], jx[s, :, pl.ds(start, width)],
                preferred_element_type=jnp.float32,
            )

            @pl.when(r == 0)
            def _():
                acc[s, :, pl.ds(start, width)] = total

            @pl.when(r != 0)
            def _():
                sb[s, r - 1, :, pl.ds(start, width)] = total.astype(jnp.bfloat16)

            return carry

        lax.fori_loop(0, half // width, body, 0)

        @pl.when(r != 0)
        def _():
            send(
                sb.at[s, r - 1], rb.at[s, n_y - 1 - r], rs_s.at[s, r - 1],
                rs_r.at[s, n_y - 1 - r], {"aux": h * n_y + c},
            ).start()

    my_rows = pl.ds(pl.multiple_of(y * chunk, chunk), chunk)

    def finish(s):
        for k in range(n_y - 1):
            send(
                sb.at[s, k], rb.at[s, k], rs_s.at[s, k], rs_r.at[s, k], at_y(1)
            ).wait_recv()
        level = occ_level(occ) + occ_level((occ + n_occ - 1 - s) % n_occ)

        def body(t, carry):
            at = pl.ds(pl.multiple_of(t * 64, 64), 64)
            left = level - vcol[pl.ds(pl.multiple_of(y * chunk + t * 64, 64), 64), :]

            def inner(u, carry):
                c = pl.ds(pl.multiple_of(u * LANES, LANES), LANES)
                there = cols(h * half + u * LANES, LANES)
                total = acc[s, at, c]
                for k in range(n_y - 1):
                    total = total + rb[s, k, at, c].astype(jnp.float32)
                divisor = left - vrow[:1, there]
                tt[s, pl.ds(pl.multiple_of(y * chunk + t * 64, 64), 64), there] = (
                    total / divisor
                ).astype(jnp.bfloat16)
                return carry

            return lax.fori_loop(0, half // LANES, inner, carry)

        lax.fori_loop(0, chunk // 64, body, 0)

    def block(s, y_at, which, lo=0, size=None):
        start = pl.multiple_of((y + y_at + n_y) % n_y * chunk + lo, sub)
        return tt.at[s, pl.ds(start, size or chunk), mine if which == 0 else other]

    def across(s):
        part = block(s, 0, 0)
        return send(part, part, ax_s.at[s], ax_r.at[s], partner)

    def across_far(s):
        part = block(s, 2, 0)
        return send(part, part, af_s.at[s], af_r.at[s], partner)

    def along(s, which, way):
        part = block(s, 0, which)
        return send(part, part, a1_s.at[s, which, way], a1_r.at[s, which, way], at_y(1 if way == 0 else n_y - 1))

    def onward(s, way):
        part = block(s, -1 if way == 0 else 1, 0, 0 if way == 0 else sub, sub)
        return send(part, part, a2_s.at[s, way], a2_r.at[s, way], at_y(1 if way == 0 else n_y - 1))

    def spread_own(s):
        across(s).start()
        along(s, 0, 0).start()
        along(s, 0, 1).start()

    def spread_partner(s):
        across(s).wait_recv()
        along(s, 1, 0).start()
        along(s, 1, 1).start()

    def forward(s):
        for way in (0, 1):
            along(s, 0, way).wait_recv()
            onward(s, way).start()

    def spread_far(s):
        for way in (0, 1):
            onward(s, way).wait_recv()
        across_far(s).start()

    def gathered(s):
        for way in (0, 1):
            along(s, 1, way).wait_recv()
        across_far(s).wait_recv()

    first, second = 0, 1

    def relay(part):
        @pl.when(core == 1)
        def _():
            ahead_parts[part].wait_recv()
            up_parts[part].start()

    def given(part):
        down_parts[part].wait_recv()

    @pl.when(core == 1)
    def _():
        given(0)
        given(1)
        for k in range(n_y // 2):
            partial_integrals(first, own_chunk(k))

    @pl.when(core == 0)
    def _():
        pl.semaphore_wait(turn_sem, 1)

        @pl.when(wraps)
        def _():
            ahead_parts[0].start()

        for k in range(n_y // 2, n_y):
            gather(k, 1 - h).start()

    for k in range(n_y // 2, n_y):
        arrived(k)
        if k == n_y - 1:
            @pl.when(core == 1)
            def _():
                pl.semaphore_signal(turn_sem, inc=1, device_id=sibling, device_id_type=MESH)

        @pl.when(core == 1)
        def _():
            partial_integrals(first, own_chunk(k))

    @pl.when(core == 0)
    def _():
        ahead_parts[0].hand_on()

    def chunks(s):
        def body(k, carry):
            partial_integrals(s, (y + k) % n_y)
            return carry

        lax.fori_loop(1, n_y + 1, body, 0)

    @pl.when(core == 0)
    def _():
        given(0)
        given(1)
        chunks(first)

    relay(0)
    relay(1)
    finish(first)
    spread_own(first)

    @pl.when(core == 1)
    def _():
        chunks(second)

    @pl.when(core == 0)
    def _():
        ahead_parts[0].wait_recv()
        ahead_parts[1].wait_recv()
        chunks(second)

    ahead_parts[2].start()
    spread_partner(first)
    forward(first)
    ahead_parts[2].hand_on()
    finish(second)
    spread_own(second)
    spread_far(first)
    relay(2)
    forward(second)
    spread_partner(second)
    gathered(first)
    given(2)

    def density(s, t):
        a_rows = pl.ds(pl.multiple_of(t * width, width), width)
        return lax.dot_general(
            jj[s], tt[s, a_rows, :], (((1,), (1,)), ((), ())), preferred_element_type=jnp.float32
        )

    def first_density(t, carry):
        g1[:, pl.ds(pl.multiple_of(t * width, width), width)] = density(first, t)
        return carry

    spread_far(second)
    lax.fori_loop(0, virt // width, first_density, 0)

    @pl.when(core == 0)
    def _():
        ahead_parts[2].wait_recv()

    gathered(second)
    per_row = virt // LANES

    def last_density(t, carry):
        total = density(second, t) + g1[:, pl.ds(pl.multiple_of(t * width, width), width)]
        for u in range(width // LANES):
            out_ref[pl.ds(t * (width // LANES) + u, rows, stride=per_row), :] = total[
                :, u * LANES : (u + 1) * LANES
            ]
        return carry

    lax.fori_loop(0, virt // width, last_density, 0)

    for k in range(n_y):
        gather(k, 1 - h).wait_send()
    for part in range(3):
        ahead_parts[part].wait_send()
        down_parts[part].wait_send()
    for s in (0, 1):
        for k in range(n_y - 1):
            send(
                sb.at[s, k], rb.at[s, k], rs_s.at[s, k], rs_r.at[s, k], at_y(1)
            ).wait_send()
        across(s).wait_send()
        across_far(s).wait_send()
        for way in (0, 1):
            along(s, 0, way).wait_send()
            along(s, 1, way).wait_send()
            onward(s, way).wait_send()


def hand_over(from_ref, to_ref):
    to_ref[...] = from_ref[...]


def on_device(factor, occ_energy, vir_energy, occ_pick, vir_pick):
    n_aux, n_occ = lax.axis_size("aux"), lax.axis_size("occ")
    n_y = n_aux // 2
    rows, _, virt = factor.shape
    half, chunk = virt // 2, virt // n_y
    bf16, f32 = jnp.bfloat16, jnp.float32
    dma = pltpu.SemaphoreType.DMA
    vmem = pl.BlockSpec(memory_space=pltpu.VMEM)
    out = pl.pallas_call(
        functools.partial(kernel, n_y, n_occ),
        out_shape=jax.ShapeDtypeStruct((rows * virt // LANES, LANES), f32),
        in_specs=[vmem, vmem, vmem, pl.BlockSpec(memory_space=pltpu.SMEM), vmem],
        out_specs=vmem,
        scratch_shapes=[
            pltpu.VMEM((rows, virt), bf16),
            pltpu.VMEM((virt, 2 * rows), bf16),
            pltpu.VMEM((3, rows, virt), bf16),
            pltpu.VMEM((2, rows, half), bf16),
            pltpu.VMEM((2, n_y - 1, chunk, half), bf16),
            pltpu.VMEM((2, n_y - 1, chunk, half), bf16),
            pltpu.VMEM((2, chunk, half), f32),
            pltpu.VMEM((2, virt, virt), bf16),
            pltpu.VMEM((rows, virt), f32),
            pltpu.VMEM((virt, LANES), f32),
            pltpu.VMEM((8, virt), f32),
            dma((n_y,)), dma((n_y,)),
            dma((3,)), dma((3,)),
            dma((3,)), dma((3,)),
            dma((3,)), dma((3,)),
            dma((3,)), dma((3,)),
            dma((2, n_y - 1)), dma((2, n_y - 1)),
            dma((2,)), dma((2,)),
            dma((2,)), dma((2,)),
            dma((2, 2, 2)), dma((2, 2, 2)),
            dma((2, 2)), dma((2, 2)),
            pltpu.SemaphoreType.REGULAR,
        ],
        compiler_params=pltpu.CompilerParams(
            collective_id=0, has_side_effects=True, vmem_limit_bytes=60 * 2**20
        ),
    )(
        factor.reshape(rows, virt),
        occ_energy.reshape(-1, LANES),
        vir_energy.reshape(-1, LANES),
        occ_pick,
        vir_pick.reshape(-1, LANES),
    )
    out = pl.pallas_call(
        hand_over,
        out_shape=jax.ShapeDtypeStruct(out.shape, f32),
        grid=(4,),
        in_specs=[pl.BlockSpec((out.shape[0] // 4, LANES), lambda i: (i, 0))],
        out_specs=pl.BlockSpec((out.shape[0] // 4, LANES), lambda i: (i, 0)),
    )(out)
    return out.reshape(rows, 1, virt)


def solution(mesh):
    placed = (P("aux", "occ", None), P(), P(), P(), P())
    return jax.shard_map(
        on_device, mesh=mesh, in_specs=placed, out_specs=P("aux", "occ", None), check_vma=False
    )
```
